32 devices in a mesh: sym: 4 (over y, core), slab: 8 (over z, x).
Axes of the slice: x: 2, y: 2, z: 4, core: 2. Of those that a mesh axis runs over, the one named last changes fastest.
Arguments:
- coefficients: float32 [8, 8192, 128], P('sym', 'slab'), may hold values from -6 to 6
- dipole: bfloat16 [8, 8192, 8192], P('sym', 'slab'), may hold values from -0.09375 to 0.09375
- energies: float32 [8, 8192], P('sym', 'slab'), may hold values from -3 to 3
- pulse_field: float32 [64], replicated, may hold values from 0.5 to 2
- live_states: int32 [8], replicated, may hold values from 4096 to 8192, as said below
Outputs:
- adjoint: float32 [8, 8192, 128], P('sym', 'slab')
The draws below stay inside these ranges and needn't reach their ends.
Inputs may be any that keep to these rules, and one draw needn't show every extreme that they name: live_states[L] counts the states in use in symmetry block L; positions at or beyond it are padding; some block uses all 8192.
All inputs are finite; a program needn't handle non-finite values.
Results may differ from the reference program's by a relative error of at most 0.0012.
Values may be sent and summed in bfloat16 or wider, within the bound.
A program may use at most 128 MiB of HBM per device.

```python
import math
import jax
import jax.numpy as jnp
from jax import lax

K = 8192
C = 64
NSYM = 8


def draw_live_states(key, part):
    counts = jax.random.randint(key, (NSYM,), K // 2, K + 1)
    full_block = jax.random.randint(jax.random.fold_in(key, 11), (), 0, NSYM)
    return counts.at[full_block].set(K).astype(jnp.int32)


def spiked(entries, key, source, target, blocks, factor):
    def block_of(axis_at):
        return (jnp.arange(entries.shape[axis_at]) // (entries.shape[axis_at] // blocks)).reshape((-1,) + (1,) * (entries.ndim - 1 - axis_at))

    one_side = jax.random.permutation(key, blocks)[block_of(target)]
    second = (block_of(target) + blocks // 2) % blocks
    return jnp.where((block_of(source) == one_side) | (block_of(source) == second), factor * entries, entries)


def steps_of(key, dims, shards, least, high):
    def one(position, parts):
        steps = jax.random.uniform(jax.random.fold_in(jax.random.fold_in(key, 6), position), (parts,), jnp.float32, least / len(shards), high / len(shards))
        return jnp.repeat(jnp.exp(steps), dims[position] // parts).reshape((-1,) + (1,) * (len(dims) - position - 1))

    gain = one(*shards[0])
    for cut in shards[1:]:
        gain = gain * one(*cut)
    return gain


def normal_values(stream_key, extent, scale, limit, shards=(), kind=jnp.bfloat16):
    result = scale * jax.random.normal(stream_key, extent, jnp.float32)
    if shards:
        result = result * steps_of(stream_key, extent, shards, -0.22, 0.18)
    return jnp.clip(result, -limit, limit).astype(kind)


def heavy_noise(own_key, extent, deviation, bound, shards, heavy, held_as=jnp.bfloat16):
    result = deviation * jax.random.normal(own_key, extent, jnp.float32)
    if shards:
        result = result * steps_of(own_key, extent, shards, -0.22, 0.18)
    return jnp.clip(spiked(result, jax.random.fold_in(own_key, 3), *heavy), -bound, bound).astype(held_as)


def setup_inputs(seed: int = 0) -> dict:
    arg_keys = jax.random.split(jax.random.key(seed), 6)
    return {
        "coefficients": normal_values(arg_keys[0], (NSYM, K, 2 * C), 1.0, 6.0, ((0, 4), (1, 8)), jnp.float32),
        "dipole": heavy_noise(arg_keys[1], (NSYM, K, K), K ** -0.5, 0.09375, ((0, 4), (1, 8)), (1, 2, 8, 2.0)),
        "energies": jnp.clip(jax.random.uniform(arg_keys[2], (NSYM, K), jnp.float32, -3.0, 3.0) * steps_of(arg_keys[2], (NSYM, K), ((0, 4), (1, 8)), -0.4, 0.0), -3.0, 3.0),
        "pulse_field": jnp.clip(jnp.exp(jax.random.uniform(arg_keys[3], (C,), jnp.float32, math.log(0.5), math.log(2.0))), 0.5, 2.0),
        "live_states": draw_live_states(jax.random.fold_in(arg_keys[5], 71), 0),
    }


step_size = 0.2


def rotate(values):
    half = values.shape[-1] // 2
    return jnp.concatenate([-values[..., half:], values[..., :half]], axis=-1)


def hamiltonian(amplitude, dipole, energies, column_gain, live_mask, upper_on):
    amplitude_bf = amplitude.astype(jnp.bfloat16)
    shifted = jnp.concatenate([amplitude_bf[1:], jnp.zeros_like(amplitude_bf[:1])], axis=0)

    def block_products(items):
        dip_block, upper_rows, own_rows = items
        forward = jnp.dot(dip_block, upper_rows, preferred_element_type=jnp.float32)
        backward = lax.dot_general(dip_block, own_rows, (((0,), (0,)), ((), ())), preferred_element_type=jnp.float32)
        return forward, backward

    forward, backward = lax.map(block_products, (dipole, shifted, amplitude_bf))
    forward = forward * upper_on[:, None, None]
    backward = backward * upper_on[:, None, None]
    lowered = jnp.concatenate([jnp.zeros_like(backward[:1]), backward[:-1]], axis=0)
    return live_mask[:, :, None] * (energies[:, :, None] * amplitude + column_gain * (forward + lowered))


def reference(coefficients, dipole, energies, pulse_field, live_states):
    positions = jnp.arange(K, dtype=jnp.int32)
    live_mask = (positions[None, :] < live_states[:, None]).astype(jnp.float32)
    block_ids = jnp.arange(NSYM, dtype=jnp.int32)
    upper_on = (block_ids < NSYM - 1).astype(jnp.float32)
    column_gain = jnp.concatenate([pulse_field, pulse_field])
    start_state = live_mask[:, :, None] * coefficients
    first_term = step_size * rotate(hamiltonian(start_state, dipole, energies, column_gain, live_mask, upper_on))
    second_term = (0.5 * step_size) * rotate(hamiltonian(first_term, dipole, energies, column_gain, live_mask, upper_on))
    return start_state + first_term + second_term
```

```python
import functools

import jax
import jax.numpy as jnp
from jax import lax
from jax.experimental import pallas as pl
from jax.experimental.pallas import tpu as pltpu
from jax.sharding import PartitionSpec as P

step_size = 0.2
MESH = pl.DeviceIdType.MESH


def ring_kernel(
    n, n_sym_dev, coef_ref, dip_ref, energy_ref, field_ref, live_ref, out_ref,
    dip, gath, rs_send, rs_recv, u_rows, u_cols, acc, state, low, low_send, low_recv,
    load_sem, start_sem, ag_send_sem, ag_recv_sem, rs_send_sem, rs_recv_sem, sym_send_sem, sym_recv_sem,
):
    n_local, cols, rows = out_ref.shape
    width = dip.shape[-1]
    half = n // 2
    side = rows // 2
    mid = cols // 2
    s = lax.axis_index("sym")
    me = lax.axis_index("slab")
    odd = me % 2
    pos = (1 - odd) * (me // 2) + odd * (n - 1 - me // 2)

    def at(offset):
        place = (pos + offset + n) % n
        back = place // half
        return (1 - back) * (2 * place) + back * (2 * (n - place) - 1)

    ring = (at(1), at(-1))
    sym_up = (s + 1) % n_sym_dev
    sym_down = (s + n_sym_dev - 1) % n_sym_dev
    sign = (1, -1)

    barrier = pltpu.get_barrier_semaphore()
    for peer in ((s, ring[0]), (s, ring[1]), (sym_up, me), (sym_down, me)):
        pl.semaphore_signal(barrier, inc=1, device_id=peer, device_id_type=MESH)

    def load(b, d):
        j = at(half + d)
        return pltpu.make_async_copy(
            dip_ref.at[b, :, pl.ds(pl.multiple_of(j * width, width), width)],
            dip.at[b, j],
            load_sem.at[b, d],
        )

    def start_load(b):
        def one(d, carry):
            load(b, d).start()
            return carry

        return one

    def wait_load(b):
        def one(d, carry):
            load(b, d).wait()
            return carry

        return one

    first_state = pltpu.make_async_copy(coef_ref, acc.at[1], start_sem)
    first_state.start()
    lax.fori_loop(0, n, start_load(0), 0)
    lax.fori_loop(0, n, start_load(1), 0)
    gain = jnp.concatenate([field_ref[...], field_ref[...]], axis=1)
    gain = jnp.broadcast_to(gain, (cols, cols)).T[:, :1]
    row_ids = me * rows + lax.broadcasted_iota(jnp.int32, (1, rows), 1)
    mask = [(row_ids < live_ref[s * 2 + b]).astype(jnp.float32) for b in range(2)]
    first_state.wait()
    for b in range(2):
        state[b] = mask[b] * acc[1, b].T

    def ag_copy(h, b, g, k, owner):
        slot = gath.at[h, b, owner]
        if k == half - 1:
            slot = gath.at[h, b, owner, pl.ds(g * side, side)]
        return pltpu.make_async_remote_copy(
            src_ref=slot, dst_ref=slot,
            send_sem=ag_send_sem.at[h, b, g, k], recv_sem=ag_recv_sem.at[h, b, g, k],
            device_id=(s, ring[g]), device_id_type=MESH,
        )

    def ag_out(h, b, g, k):
        return ag_copy(h, b, g, k, at(-sign[g] * k))

    def ag_in(h, b, g, k):
        return ag_copy(h, b, g, k, at(-sign[g] * (k + 1)))

    def rs_copy(h, b, g, k):
        source, target = rs_send.at[b, g, k], rs_recv.at[h, b, g, k]
        if k == 0:
            piece = pl.ds(g * mid, mid)
            source, target = rs_send.at[b, g, k, piece], rs_recv.at[h, b, g, k, piece]
        return pltpu.make_async_remote_copy(
            src_ref=source, dst_ref=target,
            send_sem=rs_send_sem.at[h, b, g, k], recv_sem=rs_recv_sem.at[h, b, g, k],
            device_id=(s, ring[g]), device_id_type=MESH,
        )

    def sym_rows(h):
        return pltpu.make_async_remote_copy(
            src_ref=u_rows, dst_ref=gath.at[h, 1, me],
            send_sem=sym_send_sem.at[h, 0], recv_sem=sym_recv_sem.at[h, 0],
            device_id=(sym_down, me), device_id_type=MESH,
        )

    def sym_low(h):
        return pltpu.make_async_remote_copy(
            src_ref=low_send, dst_ref=low_recv.at[h],
            send_sem=sym_send_sem.at[h, 1], recv_sem=sym_recv_sem.at[h, 1],
            device_id=(sym_up, me), device_id_type=MESH,
        )

    tile = min(256, width)
    row_tile = min(256, rows)

    def over_tiles(h, b, j, emit):
        def one(t, c):
            piece = pl.ds(pl.multiple_of(t * tile, tile), tile)
            emit(piece, jnp.dot(u_cols[h, b], dip[b, j, :, piece], preferred_element_type=jnp.float32))
            return c

        lax.fori_loop(0, width // tile, one, 0)

    def add_hop(h, b, g, k, piece, value):
        if k == 0:
            got = rs_recv[h, b, g, 0, g * mid:(g + 1) * mid, piece].astype(jnp.float32)
            parts = [value[:mid], value[mid:]]
            parts[g] = parts[g] + got
            return jnp.concatenate(parts, axis=0)
        return value + rs_recv[h, b, g, k, :, piece].astype(jnp.float32)

    def rs_free(h, b, g, k):
        if h == 1:
            rs_copy(0, b, g, k).wait_send()

    def rs_first(h, b):
        def emit(piece, value):
            value = value.astype(jnp.bfloat16)
            rs_send[b, 0, 0, :mid, piece] = value[:mid]
            rs_send[b, 1, 0, mid:, piece] = value[mid:]

        for g in range(2):
            rs_free(h, b, g, 0)
        over_tiles(h, b, at(half), emit)
        for g in range(2):
            rs_copy(h, b, g, 0).start()

    def rs_hop(h, b, g, k):
        rs_free(h, b, g, k)
        rs_copy(h, b, g, k - 1).wait_recv()

        def emit(piece, value):
            rs_send[b, g, k, :, piece] = add_hop(h, b, g, k - 1, piece, value).astype(jnp.bfloat16)

        over_tiles(h, b, at(sign[g] * (half - k)), emit)
        rs_copy(h, b, g, k).start()

    def rs_last(h, b, target):
        for g in range(2):
            rs_copy(h, b, g, half - 1).wait_recv()

        def emit(piece, value):
            for g in range(2):
                value = add_hop(h, b, g, half - 1, piece, value)
            target[:, piece] = value

        over_tiles(h, b, me, emit)

    def forward(h, b, j, first=False):
        def one(t, c):
            piece = pl.ds(pl.multiple_of(t * row_tile, row_tile), row_tile)
            value = jnp.dot(dip[b, j, piece, :], gath[h, b, j], preferred_element_type=jnp.float32)
            acc[h, b, piece, :] = value if first else acc[h, b, piece, :] + value
            return c

        lax.fori_loop(0, rows // row_tile, one, 0)

    def present(h, b):
        if b == 0:
            if h == 1:
                sym_rows(0).wait_send()
            u_rows[...] = state[0].T.astype(jnp.bfloat16)
            sym_rows(h).start()
        else:
            gath[h, 0, me] = state[1].T.astype(jnp.bfloat16)
        u_cols[h, b] = state[b].astype(jnp.bfloat16)

    def begin(h, c):
        if c == 0 and h == 1:
            for g in range(2):
                ag_out(h, 0, g, 0).start()
        rs_first(h, 1 - c)
        if c == 1:
            sym_rows(h).wait_recv()
            for g in range(2):
                ag_out(h, 1, g, 0).start()

    def finish(h, c):
        upper = acc[h, c].T
        if c == 0:
            sym_low(h).wait_recv()
            lower = low_recv[h] * (s > 0).astype(jnp.float32)
        else:
            lower = low[...]
            upper = upper * (s < n_sym_dev - 1).astype(jnp.float32)
        applied = mask[c] * (energy_ref[c:c + 1] * state[c] + gain * (upper + lower))
        turned = step_size / (h + 1) * jnp.concatenate([-applied[mid:], applied[:mid]], axis=0)
        if h == 0:
            out_ref[c] = state[c] + turned
            state[c] = turned
            present(1, c)
        else:
            out_ref[c] = out_ref[c] + turned

    lag = 2
    begins = {(0, 1): 0, (0, 0): lag, (1, 0): half, (1, 1): half + lag}
    present(0, 1)
    pl.semaphore_wait(barrier, 4)
    for g in range(2):
        ag_out(0, 0, g, 0).start()
    present(0, 0)
    for t in range(2 * half + lag + 1):
        live = [(h, c, t - begins[h, c]) for h, c in begins if 0 <= t - begins[h, c] <= half]
        for h, c, k in live:
            if k > 0:
                for g in range(2):
                    ag_in(h, c, g, k - 1).wait_recv()
                    if k < half:
                        ag_out(h, c, g, k).start()
        if t == 1:
            lax.fori_loop(1, n, wait_load(0), 0)
        for h, c, k in live:
            if 0 < k < half:
                for g in range(2):
                    rs_hop(h, 1 - c, g, k)
            if k == half:
                if c == 0:
                    if h == 1:
                        sym_low(0).wait_send()
                    rs_last(h, 1, low_send)
                    sym_low(h).start()
                else:
                    rs_last(h, 0, low)
        if t == 1:
            lax.fori_loop(0, n, wait_load(1), 0)
        for h, c, k in live:
            if k == 1:
                forward(h, c, me, first=True)
            if 0 < k < half:
                for g in range(2):
                    forward(h, c, at(-sign[g] * k))
            if k == half:
                forward(h, c, at(half))
                finish(h, c)
        for h, c, k in live:
            if k == 0:
                if t == 0:
                    load(0, 0).wait()
                begin(h, c)

    sym_rows(1).wait_send()
    sym_low(1).wait_send()
    for b in range(2):
        for g in range(2):
            for k in range(half):
                rs_copy(1, b, g, k).wait_send()
                for h in range(2):
                    ag_out(h, b, g, k).wait_send()


def ring_local(coefficients, dipole, energies, pulse_field, live_states):
    n_local, n_rows, n_cols = coefficients.shape
    assert n_local == 2
    n = lax.axis_size("slab")
    n_sym_dev = lax.axis_size("sym")
    width = dipole.shape[2] // n
    half = n // 2
    hops = (2, n_local, 2, half)
    f32, bf16 = jnp.float32, jnp.bfloat16
    vmem = pl.BlockSpec(memory_space=pltpu.VMEM)
    hbm = pl.BlockSpec(memory_space=pl.ANY)
    dma = pltpu.SemaphoreType.DMA
    flops = 8 * n_local * n_rows * dipole.shape[2] * n_cols
    adjoint = pl.pallas_call(
        functools.partial(ring_kernel, n, n_sym_dev),
        out_shape=jax.ShapeDtypeStruct((n_local, n_cols, n_rows), f32),
        in_specs=[hbm, hbm, vmem, vmem, pl.BlockSpec(memory_space=pltpu.SMEM)],
        out_specs=vmem,
        scratch_shapes=[
            pltpu.VMEM((n_local, n, n_rows, width), bf16),
            pltpu.VMEM((2, n_local, n, n_rows, n_cols), bf16),
            pltpu.VMEM((n_local, 2, half, n_cols, n_rows), bf16),
            pltpu.VMEM((2, n_local, 2, half, n_cols, n_rows), bf16),
            pltpu.VMEM((n_rows, n_cols), bf16),
            pltpu.VMEM((2, n_local, n_cols, n_rows), bf16),
            pltpu.VMEM((2, n_local, n_rows, n_cols), f32),
            pltpu.VMEM((n_local, n_cols, n_rows), f32),
            pltpu.VMEM((n_cols, n_rows), f32),
            pltpu.VMEM((n_cols, n_rows), f32),
            pltpu.VMEM((2, n_cols, n_rows), f32),
            dma((n_local, n)),
            dma,
            dma(hops), dma(hops), dma(hops), dma(hops),
            dma((2, 2)), dma((2, 2)),
        ],
        compiler_params=pltpu.CompilerParams(
            collective_id=0, has_side_effects=True, vmem_limit_bytes=62 * 2**20
        ),
        cost_estimate=pl.CostEstimate(flops=flops, bytes_accessed=2 * dipole.size, transcendentals=0),
    )(coefficients, dipole, energies, pulse_field[None, :], live_states)
    return jnp.transpose(adjoint, (0, 2, 1))


class Stream:
    def __init__(self, slot, z_first, half, rows, cols, at):
        self.slot, self.z_first, self.half = slot, z_first, half
        self.rows, self.cols, self.at = rows, cols, at


def split16(size, share):
    return min(max(int(round(size * share / 16)), 1) * 16, size - 16)


def make_streams(rows, cols):
    streams = []

    def add(slot, half, r0, r1, c0, c1, row_share, col_share, at):
        r, c = r0 + split16(r1 - r0, row_share), c0 + split16(c1 - c0, col_share)
        streams.append(Stream(slot, True, half, (r0, r), (c0, c), at[0]))
        streams.append(Stream(slot, False, half, (r, r1), (c, c1), at[1]))
        return at[0] + c - c0, at[1] + c1 - c

    add(0, None, 0, rows, 0, cols, 0.6, 0.625, (0, 0))
    at = add(1, 0, 0, rows // 2, 0, cols // 2, 0.6, 0.5, (0, 0))
    add(1, 1, rows // 2, rows, cols // 2, cols, 0.6, 0.75, at)
    return streams


def grid_kernel(
    streams, coef_ref, dip_ref, energy_ref, field_ref, live_ref, out_ref,
    big, gath, sum_z, sum_pair, from_x, last_x, u_rows, u_cols, acc, state, low, low_send, low_recv,
    load_sem, start_sem, ag_send_sem, ag_recv_sem, rs_send_sem, rs_recv_sem,
    help_send_sem, help_recv_sem, sym_send_sem, sym_recv_sem,
):
    depth, n_sym_dev = 4, 4
    n = 2 * depth
    n_local, cols, rows = out_ref.shape
    width = big.shape[-1]
    mid = cols // 2
    f32, bf16 = jnp.float32, jnp.bfloat16
    s = lax.axis_index("sym")
    me = lax.axis_index("slab")
    z, x = me // 2, me % 2
    y, core = s // 2, s % 2
    last = y * core
    other = 1 - x
    is_last, has_help = s == n_sym_dev - 1, s == 1
    halves = ((0, rows // 2, 0, mid), (rows // 2, rows - rows // 2, mid, mid))

    def both(*conditions):
        given = [c for c in conditions if c is not None]
        if not given:
            return None
        return functools.reduce(jnp.logical_and, given)

    def when(condition, do):
        if condition is None:
            do()
        else:
            pl.when(condition)(do)

    def active(q):
        half = streams[q].half
        return None if half is None else (s != n_sym_dev - 1 if half == 0 else s != 1)

    def peer_z(way):
        return (s, 2 * ((z + way + depth) % depth) + x)

    peer_x = (s, 2 * z + other)

    barrier = pltpu.get_barrier_semaphore()
    greet = [
        (z < depth - 1, peer_z(1)), (z > 0, peer_z(-1)), (None, peer_x),
        (s < n_sym_dev - 1, ((s + 1) % n_sym_dev, me)), (s > 0, ((s + n_sym_dev - 1) % n_sym_dev, me)),
        (core == 1, ((s + 2) % n_sym_dev, me)),
    ]
    for condition, peer in greet:
        when(condition, lambda peer=peer: pl.semaphore_signal(barrier, inc=1, device_id=peer, device_id_type=MESH))

    def order(i):
        high = z // 2
        near = z * (1 - high) + (depth - 1 - z) * high
        place = (3, 2, 1 - near, near)[i]
        return place * (1 - high) + (depth - 1 - place) * high

    def slab_of(i):
        return 2 * order(i // 2) + (other if i % 2 == 0 else x)

    def dip_row(b, j):
        return pl.multiple_of((b * n + j) * rows, rows)

    def load(b, i):
        j = slab_of(i)
        return pltpu.make_async_copy(
            dip_ref.at[b, :, pl.ds(pl.multiple_of(j * width, width), width)],
            big.at[pl.ds(dip_row(b, j), rows)],
            load_sem.at[b, i],
        )

    def part_row(h, b, j):
        if b == 0:
            return 2 * n * rows + j * cols
        return (1 - last) * (2 * n * rows + n * cols) + last * (n * rows + h * n * cols) + j * cols

    def part(h, b, j, c):
        return pl.ds(pl.multiple_of(part_row(h, b, j) + c[0], 16), c[1] - c[0])

    first_state = pltpu.make_async_copy(coef_ref, acc.at[1], start_sem)
    first_state.start()
    for i in range(n):
        load(0, i).start()

    def start_second():
        for i in range(n):
            load(1, i).start()

    when(s != n_sym_dev - 1, start_second)
    gain = jnp.concatenate([field_ref[...], field_ref[...]], axis=1)
    gain = jnp.broadcast_to(gain, (cols, cols)).T[:, :1]
    row_ids = me * rows + lax.broadcasted_iota(jnp.int32, (1, rows), 1)
    mask = [(row_ids < live_ref[s * 2 + b]).astype(f32) for b in range(2)]
    first_state.wait()
    for b in range(2):
        state[b] = mask[b] * acc[1, b].T

    def remote(src, dst, sems, index, peer):
        return pltpu.make_async_remote_copy(
            src_ref=src, dst_ref=dst, send_sem=sems[0].at[index], recv_sem=sems[1].at[index],
            device_id=peer, device_id_type=MESH,
        )

    ag_sems, rs_sems = (ag_send_sem, ag_recv_sem), (rs_send_sem, rs_recv_sem)
    help_sems, sym_sems = (help_send_sem, help_recv_sem), (sym_send_sem, sym_recv_sem)
    ways = (1, -1)

    def z_id(way, k):
        return (0 if way == 1 else 3) + k

    def x_id(way, k):
        return 6 + (0 if k == 0 else k if way == 1 else k + 3)

    def ag_z(h, q, way, k, place):
        t = streams[q]
        r = pl.ds(t.rows[0], t.rows[1] - t.rows[0])
        ref = gath.at[h, t.slot, 2 * place + x, r] if t.z_first else gath.at[h, t.slot, pl.ds(2 * place, 2), r]
        return remote(ref, ref, ag_sems, (h, q, z_id(way, k)), peer_z(way))

    def ag_x(h, q, way, k, place, column):
        t = streams[q]
        ref = gath.at[h, t.slot, 2 * place + column, pl.ds(t.rows[0], t.rows[1] - t.rows[0])]
        return remote(ref, ref, ag_sems, (h, q, x_id(way, k)), peer_x)

    def comes(way, k):
        return z >= k if way == 1 else z <= depth - 1 - k

    def goes(way):
        return z < depth - 1 if way == 1 else z > 0

    def ag_step(h, b, t):
        for q, st in enumerate(streams):
            if st.slot != b:
                continue
            on = active(q)
            if t == 0:
                def own(q=q, st=st):
                    if st.z_first:
                        for way in ways:
                            when(goes(way), lambda way=way: ag_z(h, q, way, 0, z).start())
                    ag_x(h, q, 1, 0, z, x).start()

                when(on, own)
            elif st.z_first:
                for way in ways:
                    if t > depth - 1:
                        continue

                    def relay(q=q, way=way):
                        place = z - way * t
                        ag_z(h, q, way, t - 1, place).wait_recv()
                        if t < depth - 1:
                            when(goes(way), lambda: ag_z(h, q, way, t, place).start())
                        ag_x(h, q, way, t, place, x).start()

                    when(both(on, comes(way, t)), relay)
            elif t == 1:
                def pair(q=q):
                    ag_x(h, q, 1, 0, z, other).wait_recv()
                    for way in ways:
                        when(goes(way), lambda way=way: ag_z(h, q, way, 0, z).start())

                when(on, pair)
            elif t <= depth:
                for way in ways:
                    def relay_pair(q=q, way=way):
                        place = z - way * (t - 1)
                        ag_z(h, q, way, t - 2, place).wait_recv()
                        if t - 1 < depth - 1:
                            when(goes(way), lambda: ag_z(h, q, way, t - 1, place).start())

                    when(both(on, comes(way, t - 1)), relay_pair)

    row_tile = min(256, rows)
    tile = min(256, width)

    def forward(h, b, j, first=False):
        def one(t, c):
            piece = pl.ds(pl.multiple_of(t * row_tile, row_tile), row_tile)
            source = pl.ds(pl.multiple_of(dip_row(b, j) + t * row_tile, row_tile), row_tile)
            value = jnp.dot(big[source, :], gath[h, b, j], preferred_element_type=f32)
            acc[h, b, piece, :] = value if first else acc[h, b, piece, :] + value
            return c

        lax.fori_loop(0, rows // row_tile, one, 0)

    def help_rows(h, way, k, place):
        r = pl.ds(halves[1][0], halves[1][1])
        ref = gath.at[h, 1, pl.ds(2 * place, 2), r]
        return remote(ref, ref, help_sems, (h, x_id(way, k) - 6), ((s + 2) % n_sym_dev, me))

    def each_at(k, do):
        for way in ways if k else ways[:1]:
            when(comes(way, k) if k else None, lambda way=way: do(way, z - way * k))

    def arrived(h, b, k):
        def one(way, place):
            for q, st in enumerate(streams):
                if st.slot == b and st.z_first:
                    when(active(q), lambda q=q: ag_x(h, q, way, k, place, other).wait_recv())
            if b == 1:
                when(is_last, lambda: help_rows(h, way, k, place).start())

        each_at(k, one)

    def multiply(h, b, k):
        def one(way, place):
            if b == 1:
                when(has_help, lambda: help_rows(h, way, k, place).wait_recv())
            forward(h, b, 2 * place + x, first=k == 0)
            forward(h, b, 2 * place + other)

        each_at(k, lambda way, place: when(None if b == 0 else s != n_sym_dev - 1, lambda: one(way, place)))

    def rs_x(h, q, i):
        t = streams[q]
        place = order(i)
        return remote(
            big.at[part(h, t.slot, 2 * place + other, t.cols)],
            from_x.at[h, t.slot, place, pl.ds(t.at, t.cols[1] - t.cols[0])],
            rs_sems, (h, q, 6 + i), peer_x,
        )

    def rs_z(h, q, way, k, place):
        t = streams[q]
        c = pl.ds(t.at, t.cols[1] - t.cols[0])
        box = sum_z if t.z_first else sum_pair
        to = depth if k == depth - 2 and way == -1 else place
        if t.z_first:
            source, target = box.at[h, t.slot, place, c], box.at[h, t.slot, to, c]
        else:
            source, target = box.at[h, t.slot, place, :, c], box.at[h, t.slot, to, :, c]
        return remote(source, target, rs_sems, (h, q, z_id(way, k)), peer_z(way))

    def rs_end(h, q, column):
        t = streams[q]
        c = pl.ds(t.at, t.cols[1] - t.cols[0])
        return remote(
            sum_pair.at[h, t.slot, z, column, c], last_x.at[h, t.slot, c], rs_sems, (h, q, 6), peer_x
        )

    def help_part(h, i):
        j = slab_of(i)
        c = halves[1][2:]
        target = n * rows + h * n * cols + j * cols + c[0]
        return remote(
            big.at[part(h, 1, j, (c[0], c[0] + c[1]))], big.at[pl.ds(pl.multiple_of(target, 16), c[1])],
            help_sems, (h, 7 + i), ((s + 2) % n_sym_dev, me),
        )

    def partial(h, b, i):
        for side in range(2):
            at = 2 * i + side
            j = slab_of(at)

            def compute(at=at, j=j, side=side):
                if h == 0:
                    if b == 0:
                        load(0, at).wait()
                else:
                    if side == 0:
                        for q, st in enumerate(streams):
                            if st.slot == b and st.z_first:
                                when(active(q), lambda q=q: rs_x(0, q, i).wait_send())
                    if b == 1:
                        when(has_help, lambda: help_part(0, at).wait_send())

                def one(t, c):
                    piece = pl.ds(pl.multiple_of(t * tile, tile), tile)
                    value = jnp.dot(u_cols[b], big[pl.ds(dip_row(b, j), rows), piece], preferred_element_type=f32)
                    big[part(h, b, j, (0, cols)), piece] = value.astype(bf16)
                    return c

                lax.fori_loop(0, width // tile, one, 0)
                if b == 1:
                    when(has_help, lambda: help_part(h, at).start())

            when(None if b == 0 else s != n_sym_dev - 1, compute)
            if b == 1:
                def take(at=at, j=j):
                    c = halves[1][2:]
                    landed = big.at[part(h, 1, j, (c[0], c[0] + c[1]))]
                    remote(landed, landed, help_sems, (h, 7 + at), ((s + 2) % n_sym_dev, me)).wait_recv()

                when(is_last, take)
            if side == 0:
                for q, st in enumerate(streams):
                    if st.slot == b and st.z_first:
                        when(active(q), lambda q=q: rs_x(h, q, i).start())

    def over_width(do):
        def one(t, c):
            do(pl.ds(pl.multiple_of(t * tile, tile), tile))
            return c

        lax.fori_loop(0, width // tile, one, 0)

    def rs_step(h, b, t):
        for q, st in enumerate(streams):
            if st.slot == b and st.z_first and t <= depth:
                def met(q=q, st=st):
                    rs_x(h, q, t - 1).wait_recv()

                when(active(q), met)
        for q, st in enumerate(streams):
            if st.slot != b or t > depth - 1:
                continue
            k = t - 1
            for way in ways:
                def hop(q=q, st=st, way=way):
                    place = z + way * (depth - 1 - k)
                    c = pl.ds(st.at, st.cols[1] - st.cols[0])
                    goes_on = z > 0 if way == 1 else z < depth - 1
                    if k > 0:
                        when(goes_on, lambda: rs_z(h, q, way, k - 1, place).wait_recv())

                    def add(piece):
                        if st.z_first:
                            value = big[part(h, b, 2 * place + x, st.cols), piece].astype(f32)
                            value = value + from_x[h, b, place, c, piece].astype(f32)
                            if k > 0:
                                value = value + jnp.where(goes_on, sum_z[h, b, place, c, piece].astype(f32), 0.0)
                            sum_z[h, b, place, c, piece] = value.astype(bf16)
                        else:
                            for column in range(2):
                                value = big[part(h, b, 2 * place + column, st.cols), piece].astype(f32)
                                if k > 0:
                                    got = sum_pair[h, b, place, column, c, piece].astype(f32)
                                    value = value + jnp.where(goes_on, got, 0.0)
                                sum_pair[h, b, place, column, c, piece] = value.astype(bf16)

                    over_width(add)
                    rs_z(h, q, way, k, place).start()

                when(both(active(q), z <= k if way == 1 else z >= depth - 1 - k), hop)

    def rs_close(h, b, target):
        for q, st in enumerate(streams):
            if st.slot != b:
                continue

            def close(q=q, st=st):
                c = pl.ds(st.at, st.cols[1] - st.cols[0])
                to = pl.ds(st.cols[0], st.cols[1] - st.cols[0])
                when(z > 0, lambda: rs_z(h, q, 1, depth - 2, z).wait_recv())
                when(z < depth - 1, lambda: rs_z(h, q, -1, depth - 2, z).wait_recv())

                def add(piece):
                    def total(column, below, above):
                        value = big[part(h, b, 2 * z + column, st.cols), piece].astype(f32)
                        value = value + jnp.where(z > 0, below.astype(f32), 0.0)
                        return value + jnp.where(z < depth - 1, above.astype(f32), 0.0)

                    if st.z_first:
                        value = total(x, sum_z[h, b, z, c, piece], sum_z[h, b, depth, c, piece])
                        target[to, piece] = value + from_x[h, b, z, c, piece].astype(f32)
                    else:
                        far = total(other, sum_pair[h, b, z, other, c, piece], sum_pair[h, b, depth, other, c, piece])
                        sum_pair[h, b, z, other, c, piece] = far.astype(bf16)
                        target[to, piece] = total(
                            x, sum_pair[h, b, z, x, c, piece], sum_pair[h, b, depth, x, c, piece]
                        )

                over_width(add)
                if not st.z_first:
                    rs_end(h, q, other).start()

            when(active(q), close)

    def rs_finish(h, b, target):
        for q, st in enumerate(streams):
            if st.slot != b or st.z_first:
                continue

            def end(q=q, st=st):
                c = pl.ds(st.at, st.cols[1] - st.cols[0])
                to = pl.ds(st.cols[0], st.cols[1] - st.cols[0])
                rs_end(h, q, x).wait_recv()

                def add(piece):
                    target[to, piece] = target[to, piece] + last_x[h, b, c, piece].astype(f32)

                over_width(add)

            when(active(q), end)

    def sym_rows(h, half):
        r = pl.ds(halves[half][0], halves[half][1])
        down = s - 1 + (0 if half == 0 else 2 * y * (1 - core))
        return remote(
            u_rows.at[r], gath.at[h, 1, me, r], sym_sems, (h, half), ((down + n_sym_dev) % n_sym_dev, me)
        )

    def sym_low(h, half):
        c = pl.ds(halves[half][2], halves[half][3])
        up = s + 1 - (0 if half == 0 else 2 * last)
        return remote(
            low_send.at[c], low_recv.at[h, c], sym_sems, (h, 2 + half), (up % n_sym_dev, me)
        )

    rows_sent = (s > 0, s > 0)
    rows_taken = (s < n_sym_dev - 1, s != 1)
    low_sent = (s < n_sym_dev - 1, s != 1)
    low_taken = (s > 0, s > 0)

    def for_halves(conditions, do):
        for half in range(2):
            when(conditions[half], lambda half=half: do(half))

    def present(h, b):
        if b == 0:
            if h == 1:
                for_halves(rows_sent, lambda half: sym_rows(0, half).wait_send())
            u_rows[...] = state[0].T.astype(bf16)
            for_halves(rows_sent, lambda half: sym_rows(h, half).start())
        else:
            gath[h, 0, me] = state[1].T.astype(bf16)
        u_cols[b] = state[b].astype(bf16)

    def finish(h, c):
        upper = acc[h, c].T
        if c == 0:
            for_halves(low_taken, lambda half: sym_low(h, half).wait_recv())
            lower = jnp.where(s > 0, low_recv[h], 0.0)
        else:
            lower = low[...]
            upper = jnp.where(s < n_sym_dev - 1, upper, 0.0)
        applied = mask[c] * (energy_ref[c:c + 1] * state[c] + gain * (upper + lower))
        turned = step_size / (h + 1) * jnp.concatenate([-applied[mid:], applied[:mid]], axis=0)
        if h == 0:
            out_ref[c] = state[c] + turned
            state[c] = turned
            present(1, c)
        else:
            out_ref[c] = out_ref[c] + turned

    span, lag = depth + 1, 2
    begins = {(0, 1): 0, (0, 0): lag, (1, 0): span, (1, 1): span + lag}
    fresh = {0: (0, 1), 1: (2,), 2: (3,)}
    u_cols[0] = state[0].astype(bf16)
    u_rows[...] = state[0].T.astype(bf16)
    pl.semaphore_wait(
        barrier,
        1 + sum((c).astype(jnp.int32) for c in (z < depth - 1, z > 0, s < n_sym_dev - 1, s > 0, core == 1)),
    )
    for_halves(rows_sent, lambda half: sym_rows(0, half).start())
    present(0, 1)

    for t in range(2 * span + lag + 1):
        live = [(h, c, t - begins[h, c]) for h, c in begins if 0 <= t - begins[h, c] <= span]
        for h, c, k in live:
            if k > 0:
                ag_step(h, c, k)
        for h, c, k in live:
            target = low if c == 1 else low_send
            if 0 < k <= depth:
                rs_step(h, 1 - c, k)
            if k == depth:
                if c == 0 and h == 1:
                    for_halves(low_sent, lambda half: sym_low(0, half).wait_send())
                rs_close(h, 1 - c, target)
            if k == span:
                rs_finish(h, 1 - c, target)
                if c == 0:
                    for_halves(low_sent, lambda half: sym_low(h, half).start())
        for h, c, k in live:
            if 0 < k <= depth:
                arrived(h, c, k - 1)
        if t == 1:
            def wait_second():
                for i in range(n):
                    load(1, i).wait()

            when(s != n_sym_dev - 1, wait_second)
        for h, c, k in live:
            if k > 0:
                for i in fresh.get(k, ()):
                    partial(h, 1 - c, i)
        for h, c, k in live:
            late = k - 1 - c
            if 0 <= late < depth:
                multiply(h, c, late)
            if k == span:
                finish(h, c)
        for h, c, k in live:
            if k == 0:
                if c == 1:
                    for_halves(rows_taken, lambda half: sym_rows(h, half).wait_recv())
                ag_step(h, c, 0)
                for i in fresh[0]:
                    partial(h, 1 - c, i)

    for_halves(rows_sent, lambda half: sym_rows(1, half).wait_send())
    for_halves(low_sent, lambda half: sym_low(1, half).wait_send())
    for h in range(2):
        for way in ways:
            for k in range(depth):
                if k == 0 and way == -1:
                    continue
                when(both(is_last, comes(way, k)), lambda: help_rows(h, way, k, z - way * k).wait_send())
        for q, st in enumerate(streams):
            def drain(q=q, st=st):
                for way in ways:
                    for k in range(depth - 1):
                        when(both(goes(way), comes(way, k)), lambda: ag_z(h, q, way, k, z - way * k).wait_send())
                        place = z + way * (depth - 1 - k)
                        when(
                            z <= k if way == 1 else z >= depth - 1 - k,
                            lambda: rs_z(h, q, way, k, place).wait_send(),
                        )
                    for k in range(1, depth):
                        if st.z_first:
                            when(comes(way, k), lambda: ag_x(h, q, way, k, z - way * k, x).wait_send())
                ag_x(h, q, 1, 0, z, x).wait_send()
                if not st.z_first:
                    rs_end(h, q, other).wait_send()
                elif h == 1:
                    for i in range(depth):
                        rs_x(1, q, i).wait_send()
                elif st.half == 1:
                    def kept():
                        for i in range(depth):
                            rs_x(0, q, i).wait_send()

                    when(is_last, kept)

            when(active(q), drain)

    def drain_help():
        for i in range(n):
            help_part(1, i).wait_send()

    when(has_help, drain_help)


def grid_local(coefficients, dipole, energies, pulse_field, live_states):
    n_local, n_rows, n_cols = coefficients.shape
    n, depth = 8, 4
    width = dipole.shape[2] // n
    f32, bf16 = jnp.float32, jnp.bfloat16
    streams = make_streams(n_rows, n_cols)
    count = len(streams)
    first = max(t.at + t.cols[1] - t.cols[0] for t in streams if t.z_first)
    second = max(t.at + t.cols[1] - t.cols[0] for t in streams if not t.z_first)
    vmem = pl.BlockSpec(memory_space=pltpu.VMEM)
    hbm = pl.BlockSpec(memory_space=pl.ANY)
    dma = pltpu.SemaphoreType.DMA
    flops = 8 * n_local * n_rows * dipole.shape[2] * n_cols
    adjoint = pl.pallas_call(
        functools.partial(grid_kernel, streams),
        out_shape=jax.ShapeDtypeStruct((n_local, n_cols, n_rows), f32),
        in_specs=[hbm, hbm, vmem, vmem, pl.BlockSpec(memory_space=pltpu.SMEM)],
        out_specs=vmem,
        scratch_shapes=[
            pltpu.VMEM((2 * n * n_rows + 2 * n * n_cols, width), bf16),
            pltpu.VMEM((2, n_local, n, n_rows, n_cols), bf16),
            pltpu.VMEM((2, n_local, depth + 1, first, n_rows), bf16),
            pltpu.VMEM((2, n_local, depth + 1, 2, second, n_rows), bf16),
            pltpu.VMEM((2, n_local, depth, first, n_rows), bf16),
            pltpu.VMEM((2, n_local, second, n_rows), bf16),
            pltpu.VMEM((n_rows, n_cols), bf16),
            pltpu.VMEM((n_local, n_cols, n_rows), bf16),
            pltpu.VMEM((2, n_local, n_rows, n_cols), f32),
            pltpu.VMEM((n_local, n_cols, n_rows), f32),
            pltpu.VMEM((n_cols, n_rows), f32),
            pltpu.VMEM((n_cols, n_rows), f32),
            pltpu.VMEM((2, n_cols, n_rows), f32),
            dma((n_local, n)),
            dma,
            dma((2, count, 13)), dma((2, count, 13)),
            dma((2, count, 10)), dma((2, count, 10)),
            dma((2, 15)), dma((2, 15)),
            dma((2, 4)), dma((2, 4)),
        ],
        compiler_params=pltpu.CompilerParams(
            collective_id=1, has_side_effects=True, vmem_limit_bytes=62 * 2**20
        ),
        cost_estimate=pl.CostEstimate(flops=flops, bytes_accessed=2 * dipole.size, transcendentals=0),
    )(coefficients, dipole, energies, pulse_field[None, :], live_states)
    return jnp.transpose(adjoint, (0, 2, 1))


def solution(mesh):
    placed = (P("sym", "slab", None), P("sym", "slab", None), P("sym", "slab"), P(), P())
    small = mesh.shape["slab"] == 8 and mesh.shape["sym"] == 4
    return jax.shard_map(
        grid_local if small else ring_local,
        mesh=mesh, in_specs=placed, out_specs=P("sym", "slab", None), check_vma=False,
    )
```

```python
import functools

import jax
import jax.numpy as jnp
from jax import lax
from jax.experimental import pallas as pl
from jax.experimental.pallas import tpu as pltpu
from jax.sharding import PartitionSpec as P

step_size = 0.2
MESH = pl.DeviceIdType.MESH


def ring_kernel(
    n, n_sym_dev, coef_ref, dip_ref, energy_ref, field_ref, live_ref, out_ref,
    dip, gath, rs_send, rs_recv, u_rows, u_cols, acc, state, low, low_send, low_recv,
    load_sem, start_sem, ag_send_sem, ag_recv_sem, rs_send_sem, rs_recv_sem, sym_send_sem, sym_recv_sem,
):
    n_local, cols, rows = out_ref.shape
    width = dip.shape[-1]
    half = n // 2
    side = rows // 2
    mid = cols // 2
    s = lax.axis_index("sym")
    me = lax.axis_index("slab")
    odd = me % 2
    pos = (1 - odd) * (me // 2) + odd * (n - 1 - me // 2)

    def at(offset):
        place = (pos + offset + n) % n
        back = place // half
        return (1 - back) * (2 * place) + back * (2 * (n - place) - 1)

    ring = (at(1), at(-1))
    sym_up = (s + 1) % n_sym_dev
    sym_down = (s + n_sym_dev - 1) % n_sym_dev
    sign = (1, -1)

    barrier = pltpu.get_barrier_semaphore()
    for peer in ((s, ring[0]), (s, ring[1]), (sym_up, me), (sym_down, me)):
        pl.semaphore_signal(barrier, inc=1, device_id=peer, device_id_type=MESH)

    def load(b, d):
        j = at(half + d)
        return pltpu.make_async_copy(
            dip_ref.at[b, :, pl.ds(pl.multiple_of(j * width, width), width)],
            dip.at[b, j],
            load_sem.at[b, d],
        )

    def start_load(b):
        def one(d, carry):
            load(b, d).start()
            return carry

        return one

    def wait_load(b):
        def one(d, carry):
            load(b, d).wait()
            return carry

        return one

    first_state = pltpu.make_async_copy(coef_ref, acc.at[1], start_sem)
    first_state.start()
    lax.fori_loop(0, n, start_load(0), 0)
    lax.fori_loop(0, n, start_load(1), 0)
    gain = jnp.concatenate([field_ref[...], field_ref[...]], axis=1)
    gain = jnp.broadcast_to(gain, (cols, cols)).T[:, :1]
    row_ids = me * rows + lax.broadcasted_iota(jnp.int32, (1, rows), 1)
    mask = [(row_ids < live_ref[s * 2 + b]).astype(jnp.float32) for b in range(2)]
    first_state.wait()
    for b in range(2):
        state[b] = mask[b] * acc[1, b].T

    def ag_copy(h, b, g, k, owner):
        slot = gath.at[h, b, owner]
        if k == half - 1:
            slot = gath.at[h, b, owner, pl.ds(g * side, side)]
        return pltpu.make_async_remote_copy(
            src_ref=slot, dst_ref=slot,
            send_sem=ag_send_sem.at[h, b, g, k], recv_sem=ag_recv_sem.at[h, b, g, k],
            device_id=(s, ring[g]), device_id_type=MESH,
        )

    def ag_out(h, b, g, k):
        return ag_copy(h, b, g, k, at(-sign[g] * k))

    def ag_in(h, b, g, k):
        return ag_copy(h, b, g, k, at(-sign[g] * (k + 1)))

    def rs_copy(h, b, g, k):
        source, target = rs_send.at[b, g, k], rs_recv.at[h, b, g, k]
        if k == 0:
            piece = pl.ds(g * mid, mid)
            source, target = rs_send.at[b, g, k, piece], rs_recv.at[h, b, g, k, piece]
        return pltpu.make_async_remote_copy(
            src_ref=source, dst_ref=target,
            send_sem=rs_send_sem.at[h, b, g, k], recv_sem=rs_recv_sem.at[h, b, g, k],
            device_id=(s, ring[g]), device_id_type=MESH,
        )

    def sym_rows(h):
        return pltpu.make_async_remote_copy(
            src_ref=u_rows, dst_ref=gath.at[h, 1, me],
            send_sem=sym_send_sem.at[h, 0], recv_sem=sym_recv_sem.at[h, 0],
            device_id=(sym_down, me), device_id_type=MESH,
        )

    def sym_low(h):
        return pltpu.make_async_remote_copy(
            src_ref=low_send, dst_ref=low_recv.at[h],
            send_sem=sym_send_sem.at[h, 1], recv_sem=sym_recv_sem.at[h, 1],
            device_id=(sym_up, me), device_id_type=MESH,
        )

    tile = min(256, width)
    row_tile = min(256, rows)

    def over_tiles(h, b, j, emit):
        def one(t, c):
            piece = pl.ds(pl.multiple_of(t * tile, tile), tile)
            emit(piece, jnp.dot(u_cols[h, b], dip[b, j, :, piece], preferred_element_type=jnp.float32))
            return c

        lax.fori_loop(0, width // tile, one, 0)

    def add_hop(h, b, g, k, piece, value):
        if k == 0:
            got = rs_recv[h, b, g, 0, g * mid:(g + 1) * mid, piece].astype(jnp.float32)
            parts = [value[:mid], value[mid:]]
            parts[g] = parts[g] + got
            return jnp.concatenate(parts, axis=0)
        return value + rs_recv[h, b, g, k, :, piece].astype(jnp.float32)

    def rs_free(h, b, g, k):
        if h == 1:
            rs_copy(0, b, g, k).wait_send()

    def rs_first(h, b):
        def emit(piece, value):
            value = value.astype(jnp.bfloat16)
            rs_send[b, 0, 0, :mid, piece] = value[:mid]
            rs_send[b, 1, 0, mid:, piece] = value[mid:]

        for g in range(2):
            rs_free(h, b, g, 0)
        over_tiles(h, b, at(half), emit)
        for g in range(2):
            rs_copy(h, b, g, 0).start()

    def rs_hop(h, b, g, k):
        rs_free(h, b, g, k)
        rs_copy(h, b, g, k - 1).wait_recv()

        def emit(piece, value):
            rs_send[b, g, k, :, piece] = add_hop(h, b, g, k - 1, piece, value).astype(jnp.bfloat16)

        over_tiles(h, b, at(sign[g] * (half - k)), emit)
        rs_copy(h, b, g, k).start()

    def rs_last(h, b, target):
        for g in range(2):
            rs_copy(h, b, g, half - 1).wait_recv()

        def emit(piece, value):
            for g in range(2):
                value = add_hop(h, b, g, half - 1, piece, value)
            target[:, piece] = value

        over_tiles(h, b, me, emit)

    def forward(h, b, j, first=False):
        def one(t, c):
            piece = pl.ds(pl.multiple_of(t * row_tile, row_tile), row_tile)
            value = jnp.dot(dip[b, j, piece, :], gath[h, b, j], preferred_element_type=jnp.float32)
            acc[h, b, piece, :] = value if first else acc[h, b, piece, :] + value
            return c

        lax.fori_loop(0, rows // row_tile, one, 0)

    def present(h, b):
        if b == 0:
            if h == 1:
                sym_rows(0).wait_send()
            u_rows[...] = state[0].T.astype(jnp.bfloat16)
            sym_rows(h).start()
        else:
            gath[h, 0, me] = state[1].T.astype(jnp.bfloat16)
        u_cols[h, b] = state[b].astype(jnp.bfloat16)

    def begin(h, c):
        if c == 0 and h == 1:
            for g in range(2):
                ag_out(h, 0, g, 0).start()
        rs_first(h, 1 - c)
        if c == 1:
            sym_rows(h).wait_recv()
            for g in range(2):
                ag_out(h, 1, g, 0).start()

    def finish(h, c):
        upper = acc[h, c].T
        if c == 0:
            sym_low(h).wait_recv()
            lower = low_recv[h] * (s > 0).astype(jnp.float32)
        else:
            lower = low[...]
            upper = upper * (s < n_sym_dev - 1).astype(jnp.float32)
        applied = mask[c] * (energy_ref[c:c + 1] * state[c] + gain * (upper + lower))
        turned = step_size / (h + 1) * jnp.concatenate([-applied[mid:], applied[:mid]], axis=0)
        if h == 0:
            out_ref[c] = state[c] + turned
            state[c] = turned
            present(1, c)
        else:
            out_ref[c] = out_ref[c] + turned

    lag = 2
    begins = {(0, 1): 0, (0, 0): lag, (1, 0): half, (1, 1): half + lag}
    present(0, 1)
    pl.semaphore_wait(barrier, 4)
    for g in range(2):
        ag_out(0, 0, g, 0).start()
    present(0, 0)
    for t in range(2 * half + lag + 1):
        live = [(h, c, t - begins[h, c]) for h, c in begins if 0 <= t - begins[h, c] <= half]
        for h, c, k in live:
            if k > 0:
                for g in range(2):
                    ag_in(h, c, g, k - 1).wait_recv()
                    if k < half:
                        ag_out(h, c, g, k).start()
        if t == 1:
            lax.fori_loop(1, n, wait_load(0), 0)
        for h, c, k in live:
            if 0 < k < half:
                for g in range(2):
                    rs_hop(h, 1 - c, g, k)
            if k == half:
                if c == 0:
                    if h == 1:
                        sym_low(0).wait_send()
                    rs_last(h, 1, low_send)
                    sym_low(h).start()
                else:
                    rs_last(h, 0, low)
        if t == 1:
            lax.fori_loop(0, n, wait_load(1), 0)
        for h, c, k in live:
            if k == 1:
                forward(h, c, me, first=True)
            if 0 < k < half:
                for g in range(2):
                    forward(h, c, at(-sign[g] * k))
            if k == half:
                forward(h, c, at(half))
                finish(h, c)
        for h, c, k in live:
            if k == 0:
                if t == 0:
                    load(0, 0).wait()
                begin(h, c)

    sym_rows(1).wait_send()
    sym_low(1).wait_send()
    for b in range(2):
        for g in range(2):
            for k in range(half):
                rs_copy(1, b, g, k).wait_send()
                for h in range(2):
                    ag_out(h, b, g, k).wait_send()


def ring_local(coefficients, dipole, energies, pulse_field, live_states):
    n_local, n_rows, n_cols = coefficients.shape
    assert n_local == 2
    n = lax.axis_size("slab")
    n_sym_dev = lax.axis_size("sym")
    width = dipole.shape[2] // n
    half = n // 2
    hops = (2, n_local, 2, half)
    f32, bf16 = jnp.float32, jnp.bfloat16
    vmem = pl.BlockSpec(memory_space=pltpu.VMEM)
    hbm = pl.BlockSpec(memory_space=pl.ANY)
    dma = pltpu.SemaphoreType.DMA
    flops = 8 * n_local * n_rows * dipole.shape[2] * n_cols
    adjoint = pl.pallas_call(
        functools.partial(ring_kernel, n, n_sym_dev),
        out_shape=jax.ShapeDtypeStruct((n_local, n_cols, n_rows), f32),
        in_specs=[hbm, hbm, vmem, vmem, pl.BlockSpec(memory_space=pltpu.SMEM)],
        out_specs=vmem,
        scratch_shapes=[
            pltpu.VMEM((n_local, n, n_rows, width), bf16),
            pltpu.VMEM((2, n_local, n, n_rows, n_cols), bf16),
            pltpu.VMEM((n_local, 2, half, n_cols, n_rows), bf16),
            pltpu.VMEM((2, n_local, 2, half, n_cols, n_rows), bf16),
            pltpu.VMEM((n_rows, n_cols), bf16),
            pltpu.VMEM((2, n_local, n_cols, n_rows), bf16),
            pltpu.VMEM((2, n_local, n_rows, n_cols), f32),
            pltpu.VMEM((n_local, n_cols, n_rows), f32),
            pltpu.VMEM((n_cols, n_rows), f32),
            pltpu.VMEM((n_cols, n_rows), f32),
            pltpu.VMEM((2, n_cols, n_rows), f32),
            dma((n_local, n)),
            dma,
            dma(hops), dma(hops), dma(hops), dma(hops),
            dma((2, 2)), dma((2, 2)),
        ],
        compiler_params=pltpu.CompilerParams(
            collective_id=0, has_side_effects=True, vmem_limit_bytes=62 * 2**20
        ),
        cost_estimate=pl.CostEstimate(flops=flops, bytes_accessed=2 * dipole.size, transcendentals=0),
    )(coefficients, dipole, energies, pulse_field[None, :], live_states)
    return jnp.transpose(adjoint, (0, 2, 1))


class Stream:
    def __init__(self, slot, z_first, half, rows, cols, at, shift):
        self.slot, self.z_first, self.half = slot, z_first, half
        self.rows, self.cols, self.at, self.shift = rows, cols, at, shift


def split16(size, share):
    return min(max(int(round(size * share / 16)), 1) * 16, size - 16)


PARTS = (
    (0, None, (0, 1), (0, 1), 0.55, 0.625, (0.5, 0.25), (0.5, 0)),
    (1, 0, (0, 0.5), (0, 0.5), 0.55, 0.75, (0, 0.5), (0, 0)),
    (1, 1, (0.5, 1), (0.5, 1), 0.7, 0.5, (0, 1), (0.25, 0)),
)
GATHER_AT = {(0, 1): 0, (0, 0): 0, (1, 0): 0, (1, 1): 0.75}
REDUCE_AT = {(0, 1): 0.5, (0, 0): 1.5, (1, 0): 1, (1, 1): 1.25}
FRESH = (0, 1, 2, 3)
ARRIVED, USED = 0, 0.25


def make_streams(rows, cols):
    streams, used = [], {}
    for slot, half, row, col, row_share, col_share, first_shift, second_shift in PARTS:
        r0, r1, c0, c1 = int(row[0] * rows), int(row[1] * rows), int(col[0] * cols), int(col[1] * cols)
        r, c = r0 + split16(r1 - r0, row_share), c0 + split16(c1 - c0, col_share)
        p, q = used.get(slot, (0, 0))
        streams.append(Stream(slot, True, half, (r0, r), (c0, c), p, first_shift))
        streams.append(Stream(slot, False, half, (r, r1), (c, c1), q, second_shift))
        used[slot] = p + c - c0, q + c1 - c
    return streams


def grid_kernel(
    streams, coef_ref, dip_ref, energy_ref, field_ref, live_ref, out_ref,
    big, gath, sum_z, sum_pair, from_x, last_x, u_rows, u_cols, acc, state, low, low_send, low_recv,
    load_sem, start_sem, ag_send_sem, ag_recv_sem, rs_send_sem, rs_recv_sem,
    help_send_sem, help_recv_sem, sym_send_sem, sym_recv_sem,
):
    depth, n_sym_dev = 4, 4
    n = 2 * depth
    n_local, cols, rows = out_ref.shape
    width = big.shape[-1]
    mid = cols // 2
    f32, bf16 = jnp.float32, jnp.bfloat16
    s = lax.axis_index("sym")
    me = lax.axis_index("slab")
    z, x = me // 2, me % 2
    y, core = s // 2, s % 2
    last = y * core
    other = 1 - x
    is_last, has_help = s == n_sym_dev - 1, s == 1
    halves = ((0, rows // 2, 0, mid), (rows // 2, rows - rows // 2, mid, mid))

    def both(*conditions):
        given = [c for c in conditions if c is not None]
        if not given:
            return None
        return functools.reduce(jnp.logical_and, given)

    def when(condition, do):
        if condition is None:
            do()
        else:
            pl.when(condition)(do)

    def active(q):
        half = streams[q].half
        return None if half is None else (s != n_sym_dev - 1 if half == 0 else s != 1)

    def peer_z(way):
        return (s, 2 * ((z + way + depth) % depth) + x)

    peer_x = (s, 2 * z + other)

    barrier = pltpu.get_barrier_semaphore()
    greet = [
        (z < depth - 1, peer_z(1)), (z > 0, peer_z(-1)), (None, peer_x),
        (s < n_sym_dev - 1, ((s + 1) % n_sym_dev, me)), (s > 0, ((s + n_sym_dev - 1) % n_sym_dev, me)),
        (core == 1, ((s + 2) % n_sym_dev, me)),
    ]
    for condition, peer in greet:
        when(condition, lambda peer=peer: pl.semaphore_signal(barrier, inc=1, device_id=peer, device_id_type=MESH))

    def order(i):
        high = z // 2
        near = z * (1 - high) + (depth - 1 - z) * high
        place = (3, 2, 1 - near, near)[i]
        return place * (1 - high) + (depth - 1 - place) * high

    def slab_of(i):
        return 2 * order(i // 2) + (other if i % 2 == 0 else x)

    def dip_row(b, j):
        return pl.multiple_of((b * n + j) * rows, rows)

    def load(b, i):
        j = slab_of(i)
        return pltpu.make_async_copy(
            dip_ref.at[b, :, pl.ds(pl.multiple_of(j * width, width), width)],
            big.at[pl.ds(dip_row(b, j), rows)],
            load_sem.at[b, i],
        )

    def part_row(h, b, j):
        if b == 0:
            return 2 * n * rows + j * cols
        return (1 - last) * (2 * n * rows + n * cols) + last * (n * rows + h * n * cols) + j * cols

    def part(h, b, j, c):
        return pl.ds(pl.multiple_of(part_row(h, b, j) + c[0], 16), c[1] - c[0])

    first_state = pltpu.make_async_copy(coef_ref, acc.at[1], start_sem)
    first_state.start()
    for i in range(n):
        load(0, i).start()

    loaded = set()

    def need(places):
        for i in places:
            if i not in loaded:
                loaded.add(i)
                load(0, i).wait()

    def start_second():
        for i in range(n):
            load(1, i).start()

    when(s != n_sym_dev - 1, start_second)
    gain = jnp.concatenate([field_ref[...], field_ref[...]], axis=1)
    gain = jnp.broadcast_to(gain, (cols, cols)).T[:, :1]
    row_ids = me * rows + lax.broadcasted_iota(jnp.int32, (1, rows), 1)
    mask = [(row_ids < live_ref[s * 2 + b]).astype(f32) for b in range(2)]
    first_state.wait()
    for b in range(2):
        state[b] = mask[b] * acc[1, b].T

    def remote(src, dst, sems, index, peer):
        return pltpu.make_async_remote_copy(
            src_ref=src, dst_ref=dst, send_sem=sems[0].at[index], recv_sem=sems[1].at[index],
            device_id=peer, device_id_type=MESH,
        )

    ag_sems, rs_sems = (ag_send_sem, ag_recv_sem), (rs_send_sem, rs_recv_sem)
    help_sems, sym_sems = (help_send_sem, help_recv_sem), (sym_send_sem, sym_recv_sem)
    ways = (1, -1)

    def z_id(way, k):
        return (0 if way == 1 else 3) + k

    def x_id(way, k):
        return 6 + (0 if k == 0 else k if way == 1 else k + 3)

    def ag_z(h, q, way, k, place):
        t = streams[q]
        r = pl.ds(t.rows[0], t.rows[1] - t.rows[0])
        ref = gath.at[h, t.slot, 2 * place + x, r] if t.z_first else gath.at[h, t.slot, pl.ds(2 * place, 2), r]
        return remote(ref, ref, ag_sems, (h, q, z_id(way, k)), peer_z(way))

    def ag_x(h, q, way, k, place, column):
        t = streams[q]
        ref = gath.at[h, t.slot, 2 * place + column, pl.ds(t.rows[0], t.rows[1] - t.rows[0])]
        return remote(ref, ref, ag_sems, (h, q, x_id(way, k)), peer_x)

    def comes(way, k):
        return z >= k if way == 1 else z <= depth - 1 - k

    def goes(way):
        return z < depth - 1 if way == 1 else z > 0

    def ag_step(h, q, t):
        st = streams[q]
        on = active(q)
        if t == 0:
            def own(q=q, st=st):
                if st.z_first:
                    for way in ways:
                        when(goes(way), lambda way=way: ag_z(h, q, way, 0, z).start())
                ag_x(h, q, 1, 0, z, x).start()

            when(on, own)
        elif st.z_first:
            for way in ways:
                if t >= depth:
                    continue

                def relay(q=q, way=way):
                    place = z - way * t
                    ag_z(h, q, way, t - 1, place).wait_recv()
                    if t < depth - 1:
                        when(goes(way), lambda: ag_z(h, q, way, t, place).start())
                    ag_x(h, q, way, t, place, x).start()

                when(both(on, comes(way, t)), relay)
        elif t == 1:
            def pair(q=q):
                ag_x(h, q, 1, 0, z, other).wait_recv()
                for way in ways:
                    when(goes(way), lambda way=way: ag_z(h, q, way, 0, z).start())

            when(on, pair)
        elif t <= depth:
            for way in ways:
                def relay_pair(q=q, way=way):
                    place = z - way * (t - 1)
                    ag_z(h, q, way, t - 2, place).wait_recv()
                    if t - 1 < depth - 1:
                        when(goes(way), lambda: ag_z(h, q, way, t - 1, place).start())

                when(both(on, comes(way, t - 1)), relay_pair)

    row_tile = rows
    tile = width
    add_tile = min(256, width)

    def forward(h, b, j, first=False):
        def one(t, c):
            piece = pl.ds(pl.multiple_of(t * row_tile, row_tile), row_tile)
            source = pl.ds(pl.multiple_of(dip_row(b, j) + t * row_tile, row_tile), row_tile)
            value = jnp.dot(big[source, :], gath[h, b, j], preferred_element_type=f32)
            acc[h, b, piece, :] = value if first else acc[h, b, piece, :] + value
            return c

        lax.fori_loop(0, rows // row_tile, one, 0)

    def help_rows(h, way, k, place):
        r = pl.ds(halves[1][0], halves[1][1])
        ref = gath.at[h, 1, pl.ds(2 * place, 2), r]
        return remote(ref, ref, help_sems, (h, x_id(way, k) - 6), ((s + 2) % n_sym_dev, me))

    def each_at(k, do):
        for way in ways if k else ways[:1]:
            when(comes(way, k) if k else None, lambda way=way: do(way, z - way * k))

    def arrived(h, b, k):
        def one(way, place):
            for q, st in enumerate(streams):
                if st.slot == b and st.z_first:
                    when(active(q), lambda q=q: ag_x(h, q, way, k, place, other).wait_recv())
            if b == 1:
                when(is_last, lambda: help_rows(h, way, k, place).start())

        each_at(k, one)

    def multiply(h, b, k):
        def one(way, place):
            if b == 1:
                when(has_help, lambda: help_rows(h, way, k, place).wait_recv())
            forward(h, b, 2 * place + x, first=k == 0)
            forward(h, b, 2 * place + other)

        if b == 0:
            need(range(n))
        each_at(k, lambda way, place: when(None if b == 0 else s != n_sym_dev - 1, lambda: one(way, place)))

    def rs_x(h, q, i):
        t = streams[q]
        place = order(i)
        return remote(
            big.at[part(h, t.slot, 2 * place + other, t.cols)],
            from_x.at[h, t.slot, place, pl.ds(t.at, t.cols[1] - t.cols[0])],
            rs_sems, (h, q, 6 + i), peer_x,
        )

    def rs_z(h, q, way, k, place):
        t = streams[q]
        c = pl.ds(t.at, t.cols[1] - t.cols[0])
        box = sum_z if t.z_first else sum_pair
        to = depth if k == depth - 2 and way == -1 else place
        if t.z_first:
            source, target = box.at[h, t.slot, place, c], box.at[h, t.slot, to, c]
        else:
            source, target = box.at[h, t.slot, place, :, c], box.at[h, t.slot, to, :, c]
        return remote(source, target, rs_sems, (h, q, z_id(way, k)), peer_z(way))

    def rs_end(h, q, column):
        t = streams[q]
        c = pl.ds(t.at, t.cols[1] - t.cols[0])
        return remote(
            sum_pair.at[h, t.slot, z, column, c], last_x.at[h, t.slot, c], rs_sems, (h, q, 6), peer_x
        )

    def help_part(h, i):
        j = slab_of(i)
        c = halves[1][2:]
        target = n * rows + h * n * cols + j * cols + c[0]
        return remote(
            big.at[part(h, 1, j, (c[0], c[0] + c[1]))], big.at[pl.ds(pl.multiple_of(target, 16), c[1])],
            help_sems, (h, 7 + i), ((s + 2) % n_sym_dev, me),
        )

    def partial(h, b, i):
        for side in range(2):
            at = 2 * i + side
            j = slab_of(at)

            def compute(at=at, j=j, side=side):
                if b == 0:
                    need((at,))
                if h == 1:
                    if side == 0:
                        for q, st in enumerate(streams):
                            if st.slot == b and st.z_first:
                                when(active(q), lambda q=q: rs_x(0, q, i).wait_send())
                    if b == 1:
                        when(has_help, lambda: help_part(0, at).wait_send())

                def one(t, c):
                    piece = pl.ds(pl.multiple_of(t * tile, tile), tile)
                    value = jnp.dot(u_cols[b], big[pl.ds(dip_row(b, j), rows), piece], preferred_element_type=f32)
                    big[part(h, b, j, (0, cols)), piece] = value.astype(bf16)
                    return c

                lax.fori_loop(0, width // tile, one, 0)
                if b == 1:
                    when(has_help, lambda: help_part(h, at).start())

            when(None if b == 0 else s != n_sym_dev - 1, compute)
            if b == 1:
                def take(at=at, j=j):
                    c = halves[1][2:]
                    landed = big.at[part(h, 1, j, (c[0], c[0] + c[1]))]
                    remote(landed, landed, help_sems, (h, 7 + at), ((s + 2) % n_sym_dev, me)).wait_recv()

                when(is_last, take)
            if side == 0:
                for q, st in enumerate(streams):
                    if st.slot == b and st.z_first:
                        when(active(q), lambda q=q: rs_x(h, q, i).start())

    def over_width(do):
        def one(t, c):
            do(pl.ds(pl.multiple_of(t * add_tile, add_tile), add_tile))
            return c

        lax.fori_loop(0, width // add_tile, one, 0)

    def rs_step(h, q, t):
        st = streams[q]
        b, k = st.slot, t - 1
        if st.z_first and t <= depth:
            when(active(q), lambda: rs_x(h, q, k).wait_recv())
        if t < depth:
            for way in ways:
                def hop(way=way):
                    place = z + way * (depth - 1 - k)
                    c = pl.ds(st.at, st.cols[1] - st.cols[0])
                    goes_on = z > 0 if way == 1 else z < depth - 1
                    if k > 0:
                        when(goes_on, lambda: rs_z(h, q, way, k - 1, place).wait_recv())

                    def add(piece):
                        if st.z_first:
                            value = big[part(h, b, 2 * place + x, st.cols), piece].astype(f32)
                            value = value + from_x[h, b, place, c, piece].astype(f32)
                            if k > 0:
                                value = value + jnp.where(goes_on, sum_z[h, b, place, c, piece].astype(f32), 0.0)
                            sum_z[h, b, place, c, piece] = value.astype(bf16)
                        else:
                            for column in range(2):
                                value = big[part(h, b, 2 * place + column, st.cols), piece].astype(f32)
                                if k > 0:
                                    got = sum_pair[h, b, place, column, c, piece].astype(f32)
                                    value = value + jnp.where(goes_on, got, 0.0)
                                sum_pair[h, b, place, column, c, piece] = value.astype(bf16)

                    over_width(add)
                    rs_z(h, q, way, k, place).start()

                when(both(active(q), z <= k if way == 1 else z >= depth - 1 - k), hop)

        if t == depth:
            target = low if b == 0 else low_send
            def close():
                c = pl.ds(st.at, st.cols[1] - st.cols[0])
                to = pl.ds(st.cols[0], st.cols[1] - st.cols[0])
                when(z > 0, lambda: rs_z(h, q, 1, depth - 2, z).wait_recv())
                when(z < depth - 1, lambda: rs_z(h, q, -1, depth - 2, z).wait_recv())

                def add(piece):
                    def total(column, below, above):
                        value = big[part(h, b, 2 * z + column, st.cols), piece].astype(f32)
                        value = value + jnp.where(z > 0, below.astype(f32), 0.0)
                        return value + jnp.where(z < depth - 1, above.astype(f32), 0.0)

                    if st.z_first:
                        value = total(x, sum_z[h, b, z, c, piece], sum_z[h, b, depth, c, piece])
                        target[to, piece] = value + from_x[h, b, z, c, piece].astype(f32)
                    else:
                        far = total(other, sum_pair[h, b, z, other, c, piece], sum_pair[h, b, depth, other, c, piece])
                        sum_pair[h, b, z, other, c, piece] = far.astype(bf16)
                        target[to, piece] = total(
                            x, sum_pair[h, b, z, x, c, piece], sum_pair[h, b, depth, x, c, piece]
                        )

                over_width(add)
                if not st.z_first:
                    rs_end(h, q, other).start()

            when(active(q), close)

        if t > depth and not st.z_first:
            target = low if b == 0 else low_send
            def end():
                c = pl.ds(st.at, st.cols[1] - st.cols[0])
                to = pl.ds(st.cols[0], st.cols[1] - st.cols[0])
                rs_end(h, q, x).wait_recv()

                def add(piece):
                    target[to, piece] = target[to, piece] + last_x[h, b, c, piece].astype(f32)

                over_width(add)

            when(active(q), end)

    def sym_rows(h, half):
        r = pl.ds(halves[half][0], halves[half][1])
        down = s - 1 + (0 if half == 0 else 2 * y * (1 - core))
        return remote(
            u_rows.at[r], gath.at[h, 1, me, r], sym_sems, (h, half), ((down + n_sym_dev) % n_sym_dev, me)
        )

    def sym_low(h, half):
        c = pl.ds(halves[half][2], halves[half][3])
        up = s + 1 - (0 if half == 0 else 2 * last)
        return remote(
            low_send.at[c], low_recv.at[h, c], sym_sems, (h, 2 + half), (up % n_sym_dev, me)
        )

    rows_sent = (s > 0, s > 0)
    rows_taken = (s < n_sym_dev - 1, s != 1)
    low_sent = (s < n_sym_dev - 1, s != 1)
    low_taken = (s > 0, s > 0)

    def for_halves(conditions, do):
        for half in range(2):
            when(conditions[half], lambda half=half: do(half))

    def present(h, b):
        if b == 0:
            if h == 1:
                for_halves(rows_sent, lambda half: sym_rows(0, half).wait_send())
            u_rows[...] = state[0].T.astype(bf16)
            for_halves(rows_sent, lambda half: sym_rows(h, half).start())
        else:
            gath[h, 0, me] = state[1].T.astype(bf16)
        u_cols[b] = state[b].astype(bf16)

    def finish(h, c):
        upper = acc[h, c].T
        if c == 0:
            for_halves(low_taken, lambda half: sym_low(h, half).wait_recv())
            lower = jnp.where(s > 0, low_recv[h], 0.0)
        else:
            lower = low[...]
            upper = jnp.where(s < n_sym_dev - 1, upper, 0.0)
        applied = mask[c] * (energy_ref[c:c + 1] * state[c] + gain * (upper + lower))
        turned = step_size / (h + 1) * jnp.concatenate([-applied[mid:], applied[:mid]], axis=0)
        if h == 0:
            out_ref[c] = state[c] + turned
            state[c] = turned
            present(1, c)
        else:
            out_ref[c] = out_ref[c] + turned

    u_cols[0] = state[0].astype(bf16)
    u_rows[...] = state[0].T.astype(bf16)
    pl.semaphore_wait(
        barrier,
        1 + sum((c).astype(jnp.int32) for c in (z < depth - 1, z > 0, s < n_sym_dev - 1, s > 0, core == 1)),
    )
    for_halves(rows_sent, lambda half: sym_rows(0, half).start())
    present(0, 1)

    def start_gather(h, c):
        if c == 1:
            for_halves(rows_taken, lambda half: sym_rows(h, half).wait_recv())
        for q, st in enumerate(streams):
            if st.slot == c:
                ag_step(h, q, 0)

    def free_low(h):
        for_halves(low_sent, lambda half: sym_low(h, half).wait_send())

    def send_low(h):
        for_halves(low_sent, lambda half: sym_low(h, half).start())

    def wait_second():
        for i in range(n):
            load(1, i).wait()

    events, ends, uses = [], {}, {}

    def event(at, rank, do, *given):
        events.append((at, rank, len(events), do, given))

    for h, c in ((0, 1), (0, 0), (1, 0), (1, 1)):
        gather_at, reduce_at = GATHER_AT[h, c], REDUCE_AT[h, c]
        if h == 1:
            gather_at, reduce_at = gather_at + ends[0, 1 - c], reduce_at + ends[0, 1 - c]
        far, late = 0, 0
        event(gather_at, 6, start_gather, h, c)
        for q, st in enumerate(streams):
            if st.slot == c:
                for t in range(1, depth + (0 if st.z_first else 1)):
                    event(gather_at + st.shift[0] + t, 0, ag_step, h, q, t)
                far = max(far, st.shift[0] - (1 if st.z_first else 0))
            else:
                for t in range(1, depth + (1 if st.z_first else 2)):
                    event(reduce_at + st.shift[1] + t, 1, rs_step, h, q, t)
                late = max(late, st.shift[1])
        if c == 0:
            if h == 1:
                event(reduce_at + depth, 0, free_low, 0)
            event(reduce_at + late + depth + 1, 1, send_low, h)
        for i in range(depth):
            event(reduce_at + FRESH[i], 3 if FRESH[i] else 7, partial, h, 1 - c, i)
            uses[h, c, i] = reduce_at + FRESH[i], reduce_at + late + (2, 3, 3, 4)[i]
            event(gather_at + far + i + 1 + ARRIVED, 2, arrived, h, c, i)
            event(gather_at + far + i + 1 + c + ARRIVED + USED, 4, multiply, h, c, i)
        ends[h, c] = max(reduce_at + depth + late + 1, gather_at + far + depth + c + ARRIVED + USED)
        event(ends[h, c], 5, finish, h, c)
    second = min(
        (at, rank) for at, rank, _, do, given in events if do in (multiply, partial) and given[1] == 1
    )
    event(second[0], second[1] - 0.5, when, s != n_sym_dev - 1, wait_second)
    for c in range(2):
        for i in range(depth):
            assert FRESH[i] < i + 1 and uses[1, c, i][0] >= uses[0, c, i][1]
        assert ends[0, 1 - c] >= uses[0, c, depth - 1][0]
    for at, rank, _, do, given in sorted(events, key=lambda e: e[:3]):
        do(*given)

    for_halves(rows_sent, lambda half: sym_rows(1, half).wait_send())
    for_halves(low_sent, lambda half: sym_low(1, half).wait_send())
    for h in range(2):
        for way in ways:
            for k in range(depth):
                if k == 0 and way == -1:
                    continue
                when(both(is_last, comes(way, k)), lambda: help_rows(h, way, k, z - way * k).wait_send())
        for q, st in enumerate(streams):
            def drain(q=q, st=st):
                for way in ways:
                    for k in range(depth - 1):
                        when(both(goes(way), comes(way, k)), lambda: ag_z(h, q, way, k, z - way * k).wait_send())
                        place = z + way * (depth - 1 - k)
                        when(
                            z <= k if way == 1 else z >= depth - 1 - k,
                            lambda: rs_z(h, q, way, k, place).wait_send(),
                        )
                    for k in range(1, depth):
                        if st.z_first:
                            when(comes(way, k), lambda: ag_x(h, q, way, k, z - way * k, x).wait_send())
                ag_x(h, q, 1, 0, z, x).wait_send()
                if not st.z_first:
                    rs_end(h, q, other).wait_send()
                elif h == 1:
                    for i in range(depth):
                        rs_x(1, q, i).wait_send()
                elif st.half == 1:
                    def kept():
                        for i in range(depth):
                            rs_x(0, q, i).wait_send()

                    when(is_last, kept)

            when(active(q), drain)

    def drain_help():
        for i in range(n):
            help_part(1, i).wait_send()

    when(has_help, drain_help)


def grid_local(coefficients, dipole, energies, pulse_field, live_states):
    n_local, n_rows, n_cols = coefficients.shape
    n, depth = 8, 4
    width = dipole.shape[2] // n
    f32, bf16 = jnp.float32, jnp.bfloat16
    streams = make_streams(n_rows, n_cols)
    count = len(streams)
    first = max(t.at + t.cols[1] - t.cols[0] for t in streams if t.z_first)
    second = max(t.at + t.cols[1] - t.cols[0] for t in streams if not t.z_first)
    vmem = pl.BlockSpec(memory_space=pltpu.VMEM)
    hbm = pl.BlockSpec(memory_space=pl.ANY)
    dma = pltpu.SemaphoreType.DMA
    flops = 8 * n_local * n_rows * dipole.shape[2] * n_cols
    adjoint = pl.pallas_call(
        functools.partial(grid_kernel, streams),
        out_shape=jax.ShapeDtypeStruct((n_local, n_cols, n_rows), f32),
        in_specs=[hbm, hbm, vmem, vmem, pl.BlockSpec(memory_space=pltpu.SMEM)],
        out_specs=vmem,
        scratch_shapes=[
            pltpu.VMEM((2 * n * n_rows + 2 * n * n_cols, width), bf16),
            pltpu.VMEM((2, n_local, n, n_rows, n_cols), bf16),
            pltpu.VMEM((2, n_local, depth + 1, first, n_rows), bf16),
            pltpu.VMEM((2, n_local, depth + 1, 2, second, n_rows), bf16),
            pltpu.VMEM((2, n_local, depth, first, n_rows), bf16),
            pltpu.VMEM((2, n_local, second, n_rows), bf16),
            pltpu.VMEM((n_rows, n_cols), bf16),
            pltpu.VMEM((n_local, n_cols, n_rows), bf16),
            pltpu.VMEM((2, n_local, n_rows, n_cols), f32),
            pltpu.VMEM((n_local, n_cols, n_rows), f32),
            pltpu.VMEM((n_cols, n_rows), f32),
            pltpu.VMEM((n_cols, n_rows), f32),
            pltpu.VMEM((2, n_cols, n_rows), f32),
            dma((n_local, n)),
            dma,
            dma((2, count, 13)), dma((2, count, 13)),
            dma((2, count, 10)), dma((2, count, 10)),
            dma((2, 15)), dma((2, 15)),
            dma((2, 4)), dma((2, 4)),
        ],
        compiler_params=pltpu.CompilerParams(
            collective_id=1, has_side_effects=True, vmem_limit_bytes=62 * 2**20
        ),
        cost_estimate=pl.CostEstimate(flops=flops, bytes_accessed=2 * dipole.size, transcendentals=0),
    )(coefficients, dipole, energies, pulse_field[None, :], live_states)
    return jnp.transpose(adjoint, (0, 2, 1))


def solution(mesh):
    placed = (P("sym", "slab", None), P("sym", "slab", None), P("sym", "slab"), P(), P())
    small = mesh.shape["slab"] == 8 and mesh.shape["sym"] == 4
    return jax.shard_map(
        grid_local if small else ring_local,
        mesh=mesh, in_specs=placed, out_specs=P("sym", "slab", None), check_vma=False,
    )
```

```python
import functools

import jax
import jax.numpy as jnp
from jax import lax
from jax.experimental import pallas as pl
from jax.experimental.pallas import tpu as pltpu
from jax.sharding import PartitionSpec as P

step_size = 0.2
MESH = pl.DeviceIdType.MESH


def ring_kernel(
    n, n_sym_dev, coef_ref, dip_ref, energy_ref, field_ref, live_ref, out_ref,
    dip, gath, rs_send, rs_recv, u_rows, u_cols, acc, state, low, low_send, low_recv,
    load_sem, start_sem, ag_send_sem, ag_recv_sem, rs_send_sem, rs_recv_sem, sym_send_sem, sym_recv_sem,
):
    n_local, cols, rows = out_ref.shape
    width = dip.shape[-1]
    half = n // 2
    side = rows // 2
    mid = cols // 2
    s = lax.axis_index("sym")
    me = lax.axis_index("slab")
    odd = me % 2
    pos = (1 - odd) * (me // 2) + odd * (n - 1 - me // 2)

    def at(offset):
        place = (pos + offset + n) % n
        back = place // half
        return (1 - back) * (2 * place) + back * (2 * (n - place) - 1)

    ring = (at(1), at(-1))
    sym_up = (s + 1) % n_sym_dev
    sym_down = (s + n_sym_dev - 1) % n_sym_dev
    sign = (1, -1)

    barrier = pltpu.get_barrier_semaphore()
    for peer in ((s, ring[0]), (s, ring[1]), (sym_up, me), (sym_down, me)):
        pl.semaphore_signal(barrier, inc=1, device_id=peer, device_id_type=MESH)

    def load(b, d):
        j = at(half + d)
        return pltpu.make_async_copy(
            dip_ref.at[b, :, pl.ds(pl.multiple_of(j * width, width), width)],
            dip.at[b, j],
            load_sem.at[b, d],
        )

    def start_load(b):
        def one(d, carry):
            load(b, d).start()
            return carry

        return one

    def wait_load(b):
        def one(d, carry):
            load(b, d).wait()
            return carry

        return one

    first_state = pltpu.make_async_copy(coef_ref, acc.at[1], start_sem)
    first_state.start()
    lax.fori_loop(0, n, start_load(0), 0)
    lax.fori_loop(0, n, start_load(1), 0)
    gain = jnp.concatenate([field_ref[...], field_ref[...]], axis=1)
    gain = jnp.broadcast_to(gain, (cols, cols)).T[:, :1]
    row_ids = me * rows + lax.broadcasted_iota(jnp.int32, (1, rows), 1)
    mask = [(row_ids < live_ref[s * 2 + b]).astype(jnp.float32) for b in range(2)]
    first_state.wait()
    for b in range(2):
        state[b] = mask[b] * acc[1, b].T

    def ag_copy(h, b, g, k, owner):
        slot = gath.at[h, b, owner]
        if k == half - 1:
            slot = gath.at[h, b, owner, pl.ds(g * side, side)]
        return pltpu.make_async_remote_copy(
            src_ref=slot, dst_ref=slot,
            send_sem=ag_send_sem.at[h, b, g, k], recv_sem=ag_recv_sem.at[h, b, g, k],
            device_id=(s, ring[g]), device_id_type=MESH,
        )

    def ag_out(h, b, g, k):
        return ag_copy(h, b, g, k, at(-sign[g] * k))

    def ag_in(h, b, g, k):
        return ag_copy(h, b, g, k, at(-sign[g] * (k + 1)))

    def rs_copy(h, b, g, k):
        source, target = rs_send.at[b, g, k], rs_recv.at[h, b, g, k]
        if k == 0:
            piece = pl.ds(g * mid, mid)
            source, target = rs_send.at[b, g, k, piece], rs_recv.at[h, b, g, k, piece]
        return pltpu.make_async_remote_copy(
            src_ref=source, dst_ref=target,
            send_sem=rs_send_sem.at[h, b, g, k], recv_sem=rs_recv_sem.at[h, b, g, k],
            device_id=(s, ring[g]), device_id_type=MESH,
        )

    def sym_rows(h):
        return pltpu.make_async_remote_copy(
            src_ref=u_rows, dst_ref=gath.at[h, 1, me],
            send_sem=sym_send_sem.at[h, 0], recv_sem=sym_recv_sem.at[h, 0],
            device_id=(sym_down, me), device_id_type=MESH,
        )

    def sym_low(h):
        return pltpu.make_async_remote_copy(
            src_ref=low_send, dst_ref=low_recv.at[h],
            send_sem=sym_send_sem.at[h, 1], recv_sem=sym_recv_sem.at[h, 1],
            device_id=(sym_up, me), device_id_type=MESH,
        )

    tile = min(256, width)
    row_tile = min(256, rows)

    def over_tiles(h, b, j, emit):
        def one(t, c):
            piece = pl.ds(pl.multiple_of(t * tile, tile), tile)
            emit(piece, jnp.dot(u_cols[h, b], dip[b, j, :, piece], preferred_element_type=jnp.float32))
            return c

        lax.fori_loop(0, width // tile, one, 0)

    def add_hop(h, b, g, k, piece, value):
        if k == 0:
            got = rs_recv[h, b, g, 0, g * mid:(g + 1) * mid, piece].astype(jnp.float32)
            parts = [value[:mid], value[mid:]]
            parts[g] = parts[g] + got
            return jnp.concatenate(parts, axis=0)
        return value + rs_recv[h, b, g, k, :, piece].astype(jnp.float32)

    def rs_free(h, b, g, k):
        if h == 1:
            rs_copy(0, b, g, k).wait_send()

    def rs_first(h, b):
        def emit(piece, value):
            value = value.astype(jnp.bfloat16)
            rs_send[b, 0, 0, :mid, piece] = value[:mid]
            rs_send[b, 1, 0, mid:, piece] = value[mid:]

        for g in range(2):
            rs_free(h, b, g, 0)
        over_tiles(h, b, at(half), emit)
        for g in range(2):
            rs_copy(h, b, g, 0).start()

    def rs_hop(h, b, g, k):
        rs_free(h, b, g, k)
        rs_copy(h, b, g, k - 1).wait_recv()

        def emit(piece, value):
            rs_send[b, g, k, :, piece] = add_hop(h, b, g, k - 1, piece, value).astype(jnp.bfloat16)

        over_tiles(h, b, at(sign[g] * (half - k)), emit)
        rs_copy(h, b, g, k).start()

    def rs_last(h, b, target):
        for g in range(2):
            rs_copy(h, b, g, half - 1).wait_recv()

        def emit(piece, value):
            for g in range(2):
                value = add_hop(h, b, g, half - 1, piece, value)
            target[:, piece] = value

        over_tiles(h, b, me, emit)

    def forward(h, b, j, first=False):
        def one(t, c):
            piece = pl.ds(pl.multiple_of(t * row_tile, row_tile), row_tile)
            value = jnp.dot(dip[b, j, piece, :], gath[h, b, j], preferred_element_type=jnp.float32)
            acc[h, b, piece, :] = value if first else acc[h, b, piece, :] + value
            return c

        lax.fori_loop(0, rows // row_tile, one, 0)

    def present(h, b):
        if b == 0:
            if h == 1:
                sym_rows(0).wait_send()
            u_rows[...] = state[0].T.astype(jnp.bfloat16)
            sym_rows(h).start()
        else:
            gath[h, 0, me] = state[1].T.astype(jnp.bfloat16)
        u_cols[h, b] = state[b].astype(jnp.bfloat16)

    def begin(h, c):
        if c == 0 and h == 1:
            for g in range(2):
                ag_out(h, 0, g, 0).start()
        rs_first(h, 1 - c)
        if c == 1:
            sym_rows(h).wait_recv()
            for g in range(2):
                ag_out(h, 1, g, 0).start()

    def finish(h, c):
        upper = acc[h, c].T
        if c == 0:
            sym_low(h).wait_recv()
            lower = low_recv[h] * (s > 0).astype(jnp.float32)
        else:
            lower = low[...]
            upper = upper * (s < n_sym_dev - 1).astype(jnp.float32)
        applied = mask[c] * (energy_ref[c:c + 1] * state[c] + gain * (upper + lower))
        turned = step_size / (h + 1) * jnp.concatenate([-applied[mid:], applied[:mid]], axis=0)
        if h == 0:
            out_ref[c] = state[c] + turned
            state[c] = turned
            present(1, c)
        else:
            out_ref[c] = out_ref[c] + turned

    lag = 2
    begins = {(0, 1): 0, (0, 0): lag, (1, 0): half, (1, 1): half + lag}
    present(0, 1)
    pl.semaphore_wait(barrier, 4)
    for g in range(2):
        ag_out(0, 0, g, 0).start()
    present(0, 0)
    for t in range(2 * half + lag + 1):
        live = [(h, c, t - begins[h, c]) for h, c in begins if 0 <= t - begins[h, c] <= half]
        for h, c, k in live:
            if k > 0:
                for g in range(2):
                    ag_in(h, c, g, k - 1).wait_recv()
                    if k < half:
                        ag_out(h, c, g, k).start()
        if t == 1:
            lax.fori_loop(1, n, wait_load(0), 0)
        for h, c, k in live:
            if 0 < k < half:
                for g in range(2):
                    rs_hop(h, 1 - c, g, k)
            if k == half:
                if c == 0:
                    if h == 1:
                        sym_low(0).wait_send()
                    rs_last(h, 1, low_send)
                    sym_low(h).start()
                else:
                    rs_last(h, 0, low)
        if t == 1:
            lax.fori_loop(0, n, wait_load(1), 0)
        for h, c, k in live:
            if k == 1:
                forward(h, c, me, first=True)
            if 0 < k < half:
                for g in range(2):
                    forward(h, c, at(-sign[g] * k))
            if k == half:
                forward(h, c, at(half))
                finish(h, c)
        for h, c, k in live:
            if k == 0:
                if t == 0:
                    load(0, 0).wait()
                begin(h, c)

    sym_rows(1).wait_send()
    sym_low(1).wait_send()
    for b in range(2):
        for g in range(2):
            for k in range(half):
                rs_copy(1, b, g, k).wait_send()
                for h in range(2):
                    ag_out(h, b, g, k).wait_send()


def ring_local(coefficients, dipole, energies, pulse_field, live_states):
    n_local, n_rows, n_cols = coefficients.shape
    assert n_local == 2
    n = lax.axis_size("slab")
    n_sym_dev = lax.axis_size("sym")
    width = dipole.shape[2] // n
    half = n // 2
    hops = (2, n_local, 2, half)
    f32, bf16 = jnp.float32, jnp.bfloat16
    vmem = pl.BlockSpec(memory_space=pltpu.VMEM)
    hbm = pl.BlockSpec(memory_space=pl.ANY)
    dma = pltpu.SemaphoreType.DMA
    flops = 8 * n_local * n_rows * dipole.shape[2] * n_cols
    adjoint = pl.pallas_call(
        functools.partial(ring_kernel, n, n_sym_dev),
        out_shape=jax.ShapeDtypeStruct((n_local, n_cols, n_rows), f32),
        in_specs=[hbm, hbm, vmem, vmem, pl.BlockSpec(memory_space=pltpu.SMEM)],
        out_specs=vmem,
        scratch_shapes=[
            pltpu.VMEM((n_local, n, n_rows, width), bf16),
            pltpu.VMEM((2, n_local, n, n_rows, n_cols), bf16),
            pltpu.VMEM((n_local, 2, half, n_cols, n_rows), bf16),
            pltpu.VMEM((2, n_local, 2, half, n_cols, n_rows), bf16),
            pltpu.VMEM((n_rows, n_cols), bf16),
            pltpu.VMEM((2, n_local, n_cols, n_rows), bf16),
            pltpu.VMEM((2, n_local, n_rows, n_cols), f32),
            pltpu.VMEM((n_local, n_cols, n_rows), f32),
            pltpu.VMEM((n_cols, n_rows), f32),
            pltpu.VMEM((n_cols, n_rows), f32),
            pltpu.VMEM((2, n_cols, n_rows), f32),
            dma((n_local, n)),
            dma,
            dma(hops), dma(hops), dma(hops), dma(hops),
            dma((2, 2)), dma((2, 2)),
        ],
        compiler_params=pltpu.CompilerParams(
            collective_id=0, has_side_effects=True, vmem_limit_bytes=62 * 2**20
        ),
        cost_estimate=pl.CostEstimate(flops=flops, bytes_accessed=2 * dipole.size, transcendentals=0),
    )(coefficients, dipole, energies, pulse_field[None, :], live_states)
    return jnp.transpose(adjoint, (0, 2, 1))


class Stream:
    def __init__(self, slot, z_first, half, rows, cols, at, shift):
        self.slot, self.z_first, self.half = slot, z_first, half
        self.rows, self.cols, self.at, self.shift = rows, cols, at, shift


def split16(size, share):
    return min(max(int(round(size * share / 16)), 1) * 16, size - 16)


PARTS = (
    (0, None, (0, 1), (0, 1), 0.55, 0.625, (0.5, 0.25), (0.5, 0)),
    (1, 0, (0, 0.5), (0, 0.5), 0.55, 0.75, (0, 0.5), (0, 0)),
    (1, 1, (0.5, 1), (0.5, 1), 0.7, 0.5, (0, 1), (0.25, 0)),
)
GATHER_AT = {(0, 1): 0, (0, 0): 0, (1, 0): 0, (1, 1): 0.75}
REDUCE_AT = {(0, 1): 0.5, (0, 0): 1.5, (1, 0): 1, (1, 1): 1.25}
FRESH = (0, 1, 2, 3)
ARRIVED, USED = 0, 0.25


def make_streams(rows, cols):
    streams, used = [], {}
    for slot, half, row, col, row_share, col_share, first_shift, second_shift in PARTS:
        r0, r1, c0, c1 = int(row[0] * rows), int(row[1] * rows), int(col[0] * cols), int(col[1] * cols)
        r, c = r0 + split16(r1 - r0, row_share), c0 + split16(c1 - c0, col_share)
        p, q = used.get(slot, (0, 0))
        streams.append(Stream(slot, True, half, (r0, r), (c0, c), p, first_shift))
        streams.append(Stream(slot, False, half, (r, r1), (c, c1), q, second_shift))
        used[slot] = p + c - c0, q + c1 - c
    return streams


def grid_kernel(
    streams, coef_ref, dip_ref, energy_ref, field_ref, live_ref, out_ref,
    big, gath, sum_z, sum_pair, from_x, last_x, u_rows, u_cols, acc, state, low, low_send, low_recv,
    load_sem, start_sem, ag_send_sem, ag_recv_sem, rs_send_sem, rs_recv_sem,
    help_send_sem, help_recv_sem, sym_send_sem, sym_recv_sem,
):
    depth, n_sym_dev = 4, 4
    n = 2 * depth
    n_local, cols, rows = out_ref.shape
    width = big.shape[-1]
    mid = cols // 2
    f32, bf16 = jnp.float32, jnp.bfloat16
    s = lax.axis_index("sym")
    me = lax.axis_index("slab")
    z, x = me // 2, me % 2
    y, core = s // 2, s % 2
    last = y * core
    other = 1 - x
    is_last, has_help = s == n_sym_dev - 1, s == 1
    halves = ((0, rows // 2, 0, mid), (rows // 2, rows - rows // 2, mid, mid))

    def both(*conditions):
        given = [c for c in conditions if c is not None]
        if not given:
            return None
        return functools.reduce(jnp.logical_and, given)

    def when(condition, do):
        if condition is None:
            do()
        else:
            pl.when(condition)(do)

    def active(q):
        half = streams[q].half
        return None if half is None else (s != n_sym_dev - 1 if half == 0 else s != 1)

    def peer_z(way):
        return (s, 2 * ((z + way + depth) % depth) + x)

    peer_x = (s, 2 * z + other)

    barrier = pltpu.get_barrier_semaphore()
    greet = [
        (z < depth - 1, peer_z(1)), (z > 0, peer_z(-1)), (None, peer_x),
        (s < n_sym_dev - 1, ((s + 1) % n_sym_dev, me)), (s > 0, ((s + n_sym_dev - 1) % n_sym_dev, me)),
        (core == 1, ((s + 2) % n_sym_dev, me)),
    ]
    for condition, peer in greet:
        when(condition, lambda peer=peer: pl.semaphore_signal(barrier, inc=1, device_id=peer, device_id_type=MESH))

    def order(i):
        high = z // 2
        near = z * (1 - high) + (depth - 1 - z) * high
        place = (3, 2, 1 - near, near)[i]
        return place * (1 - high) + (depth - 1 - place) * high

    def slab_of(i):
        return 2 * order(i // 2) + (other if i % 2 == 0 else x)

    def dip_row(b, j):
        return pl.multiple_of((b * n + j) * rows, rows)

    def load(b, i):
        j = slab_of(i)
        return pltpu.make_async_copy(
            dip_ref.at[b, :, pl.ds(pl.multiple_of(j * width, width), width)],
            big.at[pl.ds(dip_row(b, j), rows)],
            load_sem.at[b, i],
        )

    def part_row(h, b, j):
        if b == 0:
            return 2 * n * rows + j * cols
        return (1 - last) * (2 * n * rows + n * cols) + last * (n * rows + h * n * cols) + j * cols

    def part(h, b, j, c):
        return pl.ds(pl.multiple_of(part_row(h, b, j) + c[0], 16), c[1] - c[0])

    first_state = pltpu.make_async_copy(coef_ref, acc.at[1], start_sem)
    first_state.start()
    for i in range(n):
        load(0, i).start()

    loaded = set()

    def need(places):
        for i in places:
            if i not in loaded:
                loaded.add(i)
                load(0, i).wait()

    def start_second():
        for i in range(n):
            load(1, i).start()

    when(s != n_sym_dev - 1, start_second)
    gain = jnp.concatenate([field_ref[...], field_ref[...]], axis=1)
    gain = jnp.broadcast_to(gain, (cols, cols)).T[:, :1]
    row_ids = me * rows + lax.broadcasted_iota(jnp.int32, (1, rows), 1)
    mask = [(row_ids < live_ref[s * 2 + b]).astype(f32) for b in range(2)]
    first_state.wait()
    for b in range(2):
        state[b] = mask[b] * acc[1, b].T

    def remote(src, dst, sems, index, peer):
        return pltpu.make_async_remote_copy(
            src_ref=src, dst_ref=dst, send_sem=sems[0].at[index], recv_sem=sems[1].at[index],
            device_id=peer, device_id_type=MESH,
        )

    ag_sems, rs_sems = (ag_send_sem, ag_recv_sem), (rs_send_sem, rs_recv_sem)
    help_sems, sym_sems = (help_send_sem, help_recv_sem), (sym_send_sem, sym_recv_sem)
    ways = (1, -1)

    def z_id(way, k):
        return (0 if way == 1 else 3) + k

    def x_id(way, k):
        return 6 + (0 if k == 0 else k if way == 1 else k + 3)

    def ag_z(h, q, way, k, place):
        t = streams[q]
        r = pl.ds(t.rows[0], t.rows[1] - t.rows[0])
        ref = gath.at[h, t.slot, 2 * place + x, r] if t.z_first else gath.at[h, t.slot, pl.ds(2 * place, 2), r]
        return remote(ref, ref, ag_sems, (h, q, z_id(way, k)), peer_z(way))

    def ag_x(h, q, way, k, place, column):
        t = streams[q]
        ref = gath.at[h, t.slot, 2 * place + column, pl.ds(t.rows[0], t.rows[1] - t.rows[0])]
        return remote(ref, ref, ag_sems, (h, q, x_id(way, k)), peer_x)

    def comes(way, k):
        return z >= k if way == 1 else z <= depth - 1 - k

    def goes(way):
        return z < depth - 1 if way == 1 else z > 0

    def ag_step(h, q, t):
        st = streams[q]
        on = active(q)
        if t == 0:
            def own(q=q, st=st):
                if st.z_first:
                    for way in ways:
                        when(goes(way), lambda way=way: ag_z(h, q, way, 0, z).start())
                ag_x(h, q, 1, 0, z, x).start()

            when(on, own)
        elif st.z_first:
            for way in ways:
                if t >= depth:
                    continue

                def relay(q=q, way=way):
                    place = z - way * t
                    ag_z(h, q, way, t - 1, place).wait_recv()
                    if t < depth - 1:
                        when(goes(way), lambda: ag_z(h, q, way, t, place).start())
                    ag_x(h, q, way, t, place, x).start()

                when(both(on, comes(way, t)), relay)
        elif t == 1:
            def pair(q=q):
                ag_x(h, q, 1, 0, z, other).wait_recv()
                for way in ways:
                    when(goes(way), lambda way=way: ag_z(h, q, way, 0, z).start())

            when(on, pair)
        elif t <= depth:
            for way in ways:
                def relay_pair(q=q, way=way):
                    place = z - way * (t - 1)
                    ag_z(h, q, way, t - 2, place).wait_recv()
                    if t - 1 < depth - 1:
                        when(goes(way), lambda: ag_z(h, q, way, t - 1, place).start())

                when(both(on, comes(way, t - 1)), relay_pair)

    row_tile = min(512, rows)
    tile = min(512, width)
    add_tile = min(256, width)

    def forward(h, b, j, first=False):
        def one(t, c):
            piece = pl.ds(pl.multiple_of(t * row_tile, row_tile), row_tile)
            source = pl.ds(pl.multiple_of(dip_row(b, j) + t * row_tile, row_tile), row_tile)
            value = jnp.dot(big[source, :], gath[h, b, j], preferred_element_type=f32)
            acc[h, b, piece, :] = value if first else acc[h, b, piece, :] + value
            return c

        lax.fori_loop(0, rows // row_tile, one, 0)

    def help_rows(h, way, k, place):
        r = pl.ds(halves[1][0], halves[1][1])
        ref = gath.at[h, 1, pl.ds(2 * place, 2), r]
        return remote(ref, ref, help_sems, (h, x_id(way, k) - 6), ((s + 2) % n_sym_dev, me))

    def each_at(k, do):
        for way in ways if k else ways[:1]:
            when(comes(way, k) if k else None, lambda way=way: do(way, z - way * k))

    def arrived(h, b, k):
        def one(way, place):
            for q, st in enumerate(streams):
                if st.slot == b and st.z_first:
                    when(active(q), lambda q=q: ag_x(h, q, way, k, place, other).wait_recv())
            if b == 1:
                when(is_last, lambda: help_rows(h, way, k, place).start())

        each_at(k, one)

    def multiply(h, b, k):
        def one(way, place):
            if b == 1:
                when(has_help, lambda: help_rows(h, way, k, place).wait_recv())
            forward(h, b, 2 * place + x, first=k == 0)
            forward(h, b, 2 * place + other)

        if b == 0:
            need(range(n))
        each_at(k, lambda way, place: when(None if b == 0 else s != n_sym_dev - 1, lambda: one(way, place)))

    def rs_x(h, q, i):
        t = streams[q]
        place = order(i)
        return remote(
            big.at[part(h, t.slot, 2 * place + other, t.cols)],
            from_x.at[h, t.slot, place, pl.ds(t.at, t.cols[1] - t.cols[0])],
            rs_sems, (h, q, 6 + i), peer_x,
        )

    def rs_z(h, q, way, k, place):
        t = streams[q]
        c = pl.ds(t.at, t.cols[1] - t.cols[0])
        box = sum_z if t.z_first else sum_pair
        to = depth if k == depth - 2 and way == -1 else place
        if t.z_first:
            source, target = box.at[h, t.slot, place, c], box.at[h, t.slot, to, c]
        else:
            source, target = box.at[h, t.slot, place, :, c], box.at[h, t.slot, to, :, c]
        return remote(source, target, rs_sems, (h, q, z_id(way, k)), peer_z(way))

    def rs_end(h, q, column):
        t = streams[q]
        c = pl.ds(t.at, t.cols[1] - t.cols[0])
        return remote(
            sum_pair.at[h, t.slot, z, column, c], last_x.at[h, t.slot, c], rs_sems, (h, q, 6), peer_x
        )

    def help_part(h, i):
        j = slab_of(i)
        c = halves[1][2:]
        target = n * rows + h * n * cols + j * cols + c[0]
        return remote(
            big.at[part(h, 1, j, (c[0], c[0] + c[1]))], big.at[pl.ds(pl.multiple_of(target, 16), c[1])],
            help_sems, (h, 7 + i), ((s + 2) % n_sym_dev, me),
        )

    def partial(h, b, i):
        for side in range(2):
            at = 2 * i + side
            j = slab_of(at)

            def compute(at=at, j=j, side=side):
                if b == 0:
                    need((at,))
                if h == 1:
                    if side == 0:
                        for q, st in enumerate(streams):
                            if st.slot == b and st.z_first:
                                when(active(q), lambda q=q: rs_x(0, q, i).wait_send())
                    if b == 1:
                        when(has_help, lambda: help_part(0, at).wait_send())

                def one(t, c):
                    piece = pl.ds(pl.multiple_of(t * tile, tile), tile)
                    value = jnp.dot(u_cols[b], big[pl.ds(dip_row(b, j), rows), piece], preferred_element_type=f32)
                    big[part(h, b, j, (0, cols)), piece] = value.astype(bf16)
                    return c

                lax.fori_loop(0, width // tile, one, 0)
                if b == 1:
                    when(has_help, lambda: help_part(h, at).start())

            when(None if b == 0 else s != n_sym_dev - 1, compute)
            if b == 1:
                def take(at=at, j=j):
                    c = halves[1][2:]
                    landed = big.at[part(h, 1, j, (c[0], c[0] + c[1]))]
                    remote(landed, landed, help_sems, (h, 7 + at), ((s + 2) % n_sym_dev, me)).wait_recv()

                when(is_last, take)
            if side == 0:
                for q, st in enumerate(streams):
                    if st.slot == b and st.z_first:
                        when(active(q), lambda q=q: rs_x(h, q, i).start())

    def over_width(do):
        def one(t, c):
            do(pl.ds(pl.multiple_of(t * add_tile, add_tile), add_tile))
            return c

        lax.fori_loop(0, width // add_tile, one, 0)

    def rs_step(h, q, t):
        st = streams[q]
        b, k = st.slot, t - 1
        if st.z_first and t <= depth:
            when(active(q), lambda: rs_x(h, q, k).wait_recv())
        if t < depth:
            for way in ways:
                def hop(way=way):
                    place = z + way * (depth - 1 - k)
                    c = pl.ds(st.at, st.cols[1] - st.cols[0])
                    goes_on = z > 0 if way == 1 else z < depth - 1
                    if k > 0:
                        when(goes_on, lambda: rs_z(h, q, way, k - 1, place).wait_recv())

                    def add(piece):
                        if st.z_first:
                            value = big[part(h, b, 2 * place + x, st.cols), piece].astype(f32)
                            value = value + from_x[h, b, place, c, piece].astype(f32)
                            if k > 0:
                                value = value + jnp.where(goes_on, sum_z[h, b, place, c, piece].astype(f32), 0.0)
                            sum_z[h, b, place, c, piece] = value.astype(bf16)
                        else:
                            for column in range(2):
                                value = big[part(h, b, 2 * place + column, st.cols), piece].astype(f32)
                                if k > 0:
                                    got = sum_pair[h, b, place, column, c, piece].astype(f32)
                                    value = value + jnp.where(goes_on, got, 0.0)
                                sum_pair[h, b, place, column, c, piece] = value.astype(bf16)

                    over_width(add)
                    rs_z(h, q, way, k, place).start()

                when(both(active(q), z <= k if way == 1 else z >= depth - 1 - k), hop)

        if t == depth:
            target = low if b == 0 else low_send
            def close():
                c = pl.ds(st.at, st.cols[1] - st.cols[0])
                to = pl.ds(st.cols[0], st.cols[1] - st.cols[0])
                when(z > 0, lambda: rs_z(h, q, 1, depth - 2, z).wait_recv())
                when(z < depth - 1, lambda: rs_z(h, q, -1, depth - 2, z).wait_recv())

                def add(piece):
                    def total(column, below, above):
                        value = big[part(h, b, 2 * z + column, st.cols), piece].astype(f32)
                        value = value + jnp.where(z > 0, below.astype(f32), 0.0)
                        return value + jnp.where(z < depth - 1, above.astype(f32), 0.0)

                    if st.z_first:
                        value = total(x, sum_z[h, b, z, c, piece], sum_z[h, b, depth, c, piece])
                        target[to, piece] = value + from_x[h, b, z, c, piece].astype(f32)
                    else:
                        far = total(other, sum_pair[h, b, z, other, c, piece], sum_pair[h, b, depth, other, c, piece])
                        sum_pair[h, b, z, other, c, piece] = far.astype(bf16)
                        target[to, piece] = total(
                            x, sum_pair[h, b, z, x, c, piece], sum_pair[h, b, depth, x, c, piece]
                        )

                over_width(add)
                if not st.z_first:
                    rs_end(h, q, other).start()

            when(active(q), close)

        if t > depth and not st.z_first:
            target = low if b == 0 else low_send
            def end():
                c = pl.ds(st.at, st.cols[1] - st.cols[0])
                to = pl.ds(st.cols[0], st.cols[1] - st.cols[0])
                rs_end(h, q, x).wait_recv()

                def add(piece):
                    target[to, piece] = target[to, piece] + last_x[h, b, c, piece].astype(f32)

                over_width(add)

            when(active(q), end)

    def sym_rows(h, half):
        r = pl.ds(halves[half][0], halves[half][1])
        down = s - 1 + (0 if half == 0 else 2 * y * (1 - core))
        return remote(
            u_rows.at[r], gath.at[h, 1, me, r], sym_sems, (h, half), ((down + n_sym_dev) % n_sym_dev, me)
        )

    def sym_low(h, half):
        c = pl.ds(halves[half][2], halves[half][3])
        up = s + 1 - (0 if half == 0 else 2 * last)
        return remote(
            low_send.at[c], low_recv.at[h, c], sym_sems, (h, 2 + half), (up % n_sym_dev, me)
        )

    rows_sent = (s > 0, s > 0)
    rows_taken = (s < n_sym_dev - 1, s != 1)
    low_sent = (s < n_sym_dev - 1, s != 1)
    low_taken = (s > 0, s > 0)

    def for_halves(conditions, do):
        for half in range(2):
            when(conditions[half], lambda half=half: do(half))

    def present(h, b):
        if b == 0:
            if h == 1:
                for_halves(rows_sent, lambda half: sym_rows(0, half).wait_send())
            u_rows[...] = state[0].T.astype(bf16)
            for_halves(rows_sent, lambda half: sym_rows(h, half).start())
        else:
            gath[h, 0, me] = state[1].T.astype(bf16)
        u_cols[b] = state[b].astype(bf16)

    def finish(h, c):
        upper = acc[h, c].T
        if c == 0:
            for_halves(low_taken, lambda half: sym_low(h, half).wait_recv())
            lower = jnp.where(s > 0, low_recv[h], 0.0)
        else:
            lower = low[...]
            upper = jnp.where(s < n_sym_dev - 1, upper, 0.0)
        applied = mask[c] * (energy_ref[c:c + 1] * state[c] + gain * (upper + lower))
        turned = step_size / (h + 1) * jnp.concatenate([-applied[mid:], applied[:mid]], axis=0)
        if h == 0:
            out_ref[c] = state[c] + turned
            state[c] = turned
            present(1, c)
        else:
            out_ref[c] = out_ref[c] + turned

    u_cols[0] = state[0].astype(bf16)
    u_rows[...] = state[0].T.astype(bf16)
    pl.semaphore_wait(
        barrier,
        1 + sum((c).astype(jnp.int32) for c in (z < depth - 1, z > 0, s < n_sym_dev - 1, s > 0, core == 1)),
    )
    for_halves(rows_sent, lambda half: sym_rows(0, half).start())
    present(0, 1)

    def start_gather(h, c):
        if c == 1:
            for_halves(rows_taken, lambda half: sym_rows(h, half).wait_recv())
        for q, st in enumerate(streams):
            if st.slot == c:
                ag_step(h, q, 0)

    def free_low(h):
        for_halves(low_sent, lambda half: sym_low(h, half).wait_send())

    def send_low(h):
        for_halves(low_sent, lambda half: sym_low(h, half).start())

    def wait_second():
        for i in range(n):
            load(1, i).wait()

    events, ends, uses = [], {}, {}

    def event(at, rank, do, *given):
        events.append((at, rank, len(events), do, given))

    for h, c in ((0, 1), (0, 0), (1, 0), (1, 1)):
        gather_at, reduce_at = GATHER_AT[h, c], REDUCE_AT[h, c]
        if h == 1:
            gather_at, reduce_at = gather_at + ends[0, 1 - c], reduce_at + ends[0, 1 - c]
        far, late = 0, 0
        event(gather_at, 6, start_gather, h, c)
        for q, st in enumerate(streams):
            if st.slot == c:
                for t in range(1, depth + (0 if st.z_first else 1)):
                    event(gather_at + st.shift[0] + t, 0, ag_step, h, q, t)
                far = max(far, st.shift[0] - (1 if st.z_first else 0))
            else:
                for t in range(1, depth + (1 if st.z_first else 2)):
                    event(reduce_at + st.shift[1] + t, 1, rs_step, h, q, t)
                late = max(late, st.shift[1])
        if c == 0:
            if h == 1:
                event(reduce_at + depth, 0, free_low, 0)
            event(reduce_at + late + depth + 1, 1, send_low, h)
        for i in range(depth):
            event(reduce_at + FRESH[i], 3 if FRESH[i] else 7, partial, h, 1 - c, i)
            uses[h, c, i] = reduce_at + FRESH[i], reduce_at + late + (2, 3, 3, 4)[i]
            event(gather_at + far + i + 1 + ARRIVED, 2, arrived, h, c, i)
            event(gather_at + far + i + 1 + c + ARRIVED + USED, 4, multiply, h, c, i)
        ends[h, c] = max(reduce_at + depth + late + 1, gather_at + far + depth + c + ARRIVED + USED)
        event(ends[h, c], 5, finish, h, c)
    second = min(
        (at, rank) for at, rank, _, do, given in events if do in (multiply, partial) and given[1] == 1
    )
    event(second[0], second[1] - 0.5, when, s != n_sym_dev - 1, wait_second)
    for c in range(2):
        for i in range(depth):
            assert FRESH[i] < i + 1 and uses[1, c, i][0] >= uses[0, c, i][1]
        assert ends[0, 1 - c] >= uses[0, c, depth - 1][0]
    for at, rank, _, do, given in sorted(events, key=lambda e: e[:3]):
        do(*given)

    for_halves(rows_sent, lambda half: sym_rows(1, half).wait_send())
    for_halves(low_sent, lambda half: sym_low(1, half).wait_send())
    for h in range(2):
        for way in ways:
            for k in range(depth):
                if k == 0 and way == -1:
                    continue
                when(both(is_last, comes(way, k)), lambda: help_rows(h, way, k, z - way * k).wait_send())
        for q, st in enumerate(streams):
            def drain(q=q, st=st):
                for way in ways:
                    for k in range(depth - 1):
                        when(both(goes(way), comes(way, k)), lambda: ag_z(h, q, way, k, z - way * k).wait_send())
                        place = z + way * (depth - 1 - k)
                        when(
                            z <= k if way == 1 else z >= depth - 1 - k,
                            lambda: rs_z(h, q, way, k, place).wait_send(),
                        )
                    for k in range(1, depth):
                        if st.z_first:
                            when(comes(way, k), lambda: ag_x(h, q, way, k, z - way * k, x).wait_send())
                ag_x(h, q, 1, 0, z, x).wait_send()
                if not st.z_first:
                    rs_end(h, q, other).wait_send()
                elif h == 1:
                    for i in range(depth):
                        rs_x(1, q, i).wait_send()
                elif st.half == 1:
                    def kept():
                        for i in range(depth):
                            rs_x(0, q, i).wait_send()

                    when(is_last, kept)

            when(active(q), drain)

    def drain_help():
        for i in range(n):
            help_part(1, i).wait_send()

    when(has_help, drain_help)


def grid_local(coefficients, dipole, energies, pulse_field, live_states):
    n_local, n_rows, n_cols = coefficients.shape
    n, depth = 8, 4
    width = dipole.shape[2] // n
    f32, bf16 = jnp.float32, jnp.bfloat16
    streams = make_streams(n_rows, n_cols)
    count = len(streams)
    first = max(t.at + t.cols[1] - t.cols[0] for t in streams if t.z_first)
    second = max(t.at + t.cols[1] - t.cols[0] for t in streams if not t.z_first)
    vmem = pl.BlockSpec(memory_space=pltpu.VMEM)
    hbm = pl.BlockSpec(memory_space=pl.ANY)
    dma = pltpu.SemaphoreType.DMA
    flops = 8 * n_local * n_rows * dipole.shape[2] * n_cols
    adjoint = pl.pallas_call(
        functools.partial(grid_kernel, streams),
        out_shape=jax.ShapeDtypeStruct((n_local, n_cols, n_rows), f32),
        in_specs=[hbm, hbm, vmem, vmem, pl.BlockSpec(memory_space=pltpu.SMEM)],
        out_specs=vmem,
        scratch_shapes=[
            pltpu.VMEM((2 * n * n_rows + 2 * n * n_cols, width), bf16),
            pltpu.VMEM((2, n_local, n, n_rows, n_cols), bf16),
            pltpu.VMEM((2, n_local, depth + 1, first, n_rows), bf16),
            pltpu.VMEM((2, n_local, depth + 1, 2, second, n_rows), bf16),
            pltpu.VMEM((2, n_local, depth, first, n_rows), bf16),
            pltpu.VMEM((2, n_local, second, n_rows), bf16),
            pltpu.VMEM((n_rows, n_cols), bf16),
            pltpu.VMEM((n_local, n_cols, n_rows), bf16),
            pltpu.VMEM((2, n_local, n_rows, n_cols), f32),
            pltpu.VMEM((n_local, n_cols, n_rows), f32),
            pltpu.VMEM((n_cols, n_rows), f32),
            pltpu.VMEM((n_cols, n_rows), f32),
            pltpu.VMEM((2, n_cols, n_rows), f32),
            dma((n_local, n)),
            dma,
            dma((2, count, 13)), dma((2, count, 13)),
            dma((2, count, 10)), dma((2, count, 10)),
            dma((2, 15)), dma((2, 15)),
            dma((2, 4)), dma((2, 4)),
        ],
        compiler_params=pltpu.CompilerParams(
            collective_id=1, has_side_effects=True, vmem_limit_bytes=62 * 2**20
        ),
        cost_estimate=pl.CostEstimate(flops=flops, bytes_accessed=2 * dipole.size, transcendentals=0),
    )(coefficients, dipole, energies, pulse_field[None, :], live_states)
    return jnp.transpose(adjoint, (0, 2, 1))


def solution(mesh):
    placed = (P("sym", "slab", None), P("sym", "slab", None), P("sym", "slab"), P(), P())
    small = mesh.shape["slab"] == 8 and mesh.shape["sym"] == 4
    return jax.shard_map(
        grid_local if small else ring_local,
        mesh=mesh, in_specs=placed, out_specs=P("sym", "slab", None), check_vma=False,
    )
```
